256 devices in a mesh: seq: 32 (over z, x), mp: 8 (over y, core).
Axes of the slice: x: 4, y: 4, z: 8, core: 2. Of those that a mesh axis runs over, the one named last changes fastest.
Arguments:
- win_query: bfloat16 [16384, 4096], P('seq', 'mp'), may hold values from -8 to 8
- win_key: bfloat16 [16384, 4096], P('seq', 'mp'), may hold values from -8 to 8
- win_value: bfloat16 [16384, 4096], P('seq', 'mp'), may hold values from -6 to 6
- win_dout: bfloat16 [16384, 4096], P('seq', 'mp'), may hold values from -16 to 16
- cross_query: bfloat16 [16384, 4096], P('seq', 'mp'), may hold values from -8 to 8
- cross_dout: bfloat16 [16384, 4096], P('seq', 'mp'), may hold values from -16 to 16
- patch_key: bfloat16 [4096, 4096], P('seq', 'mp'), may hold values from -8 to 8
- patch_value: bfloat16 [4096, 4096], P('seq', 'mp'), may hold values from -6 to 6
- patch_len: int32 [64, 64], P('seq'), may hold values from 1 to 16, 256 in all within a row
- patch_owner: int32 [4096, 1], P('seq'), may hold values from 0 to 31; in each aligned block of 128 rows (0 to 127, 128 to 255, ...) at most 8 rows name the same one
- w_query: bfloat16 [4096, 4096], P('seq', 'mp'), may hold values from -0.09375 to 0.09375
Outputs:
- win_dq: bfloat16 [16384, 4096], P('seq', 'mp')
- win_dk: bfloat16 [16384, 4096], P('seq', 'mp')
- win_dv: bfloat16 [16384, 4096], P('seq', 'mp')
- patch_grads: bfloat16 [2, 8192, 4096], P(None, 'seq', 'mp')
- byte_grads: bfloat16 [16384, 4096], P('seq', 'mp')
The draws below stay inside these ranges and needn't reach their ends.
Inputs may be any that keep to these rules, and one draw needn't show every extreme that they name: `patch_len`: each row lists the byte lengths of the patches of one stored block in order; they sum to 256 and the largest is exactly 16. `patch_owner`: within each aligned block of 128 rows (the patch rows of one device) no owner is named more than 8 times, a bound that some block reaches.
All inputs are finite; a program needn't handle non-finite values.
Results may differ from the reference program's by a relative error of at most 0.017.
Values may be sent and summed in bfloat16 or wider, within the bound.
No kernel may reach another device: no remote copies, remote signals or barrier semaphores. Data moves between devices by JAX's collectives and lax.ppermute only.
A program may use at most 64 MiB of HBM per device.

```python
import math
import jax
import jax.numpy as jnp
import numpy as np
from jax import lax

D = 4096
HEADS = 32
HD = 128
WIN = 256
LMAX = 16
BLK = 256
PB = 64
BLOCKS = 64
BYTES = 16384
PATCHES = 4096
CAP = 8
SLOTS = 8192
N_SEQ = 32
N_MP = 8


def noise_rows(key, salt, row_count, width):
    base_key = jax.random.fold_in(key, salt)
    return jax.random.truncated_normal(base_key, -6.0, 6.0, (row_count, width), jnp.float32)


def draw_win_query(key, part):
    width = HEADS * HD
    values = noise_rows(key, 31, BYTES, width)
    return values.astype(jnp.bfloat16)


def draw_win_key(key, part):
    width = HEADS * HD
    values = noise_rows(key, 32, BYTES, width)
    return values.astype(jnp.bfloat16)


def draw_cross_query(key, part):
    width = HEADS * HD
    values = noise_rows(key, 41, BYTES, width)
    return values.astype(jnp.bfloat16)


def draw_patch_key(key, part):
    width = HEADS * HD
    values = noise_rows(key, 42, PATCHES, width)
    return values.astype(jnp.bfloat16)


def shard_levels(stream_key, shape, pieces, least, largest):
    def one(dim, parts):
        steps = jax.random.uniform(jax.random.fold_in(jax.random.fold_in(stream_key, 6), dim), (parts,), jnp.float32, least / len(pieces), largest / len(pieces))
        return jnp.repeat(jnp.exp(steps), shape[dim] // parts).reshape((-1,) + (1,) * (len(shape) - dim - 1))

    level = one(*pieces[0])
    for cut in pieces[1:]:
        level = level * one(*cut)
    return level


def length_profile(amount, total, most, lean):
    weights = [(1 << 20) // math.isqrt(rank ** lean) + 1 for rank in range(2, amount + 1)]
    rest, counts = total - most - (amount - 1), [1] * (amount - 1)
    while rest > 0:
        movable = [i for i in range(amount - 1) if counts[i] < most]
        pool, left = sum([weights[i] for i in movable]), rest
        for i in movable:
            more = min(most - counts[i], max(1, left * weights[i] // pool), rest)
            counts[i] = counts[i] + more
            rest = rest - more
    return np.array([most] + counts)


def ragged(own_key, number_of, total, reach, skew):
    if number_of == 2:
        one = jax.random.randint(own_key, (), max(1, total - reach), min(reach, total - 1) + 1)
        return jnp.stack([one, total - one])
    tallies = jnp.asarray(length_profile(number_of, total, reach, skew), jnp.int32)
    pairs = (number_of - 1) // 2
    donor, sink = tallies[1:1 + 2 * pairs:2], tallies[2:2 + 2 * pairs:2]
    margin = jnp.minimum(donor - 1, reach - sink)
    passed = jax.random.randint(jax.random.fold_in(own_key, 1), (pairs,), 0, 1 << 20) % (margin + 1)
    tallies = tallies.at[1:1 + 2 * pairs:2].set(donor - passed).at[2:2 + 2 * pairs:2].set(sink + passed)
    return tallies[jax.random.permutation(jax.random.fold_in(own_key, 2), number_of)]


def shared_out(rng, own, number, rows, amount, top, limit, lean):
    sequence = jax.random.permutation(rng, amount)
    heavy_load, common = load_shares(amount, rows * top, limit, lean, True), load_shares(amount, rows * top, limit, lean, False)
    places = jnp.arange(amount)

    def named(lengths, turn):
        used = int((lengths > 0).sum())
        fixed = max(1, used // 4)
        shifted = fixed + (places - fixed + turn * (used - fixed)) % max(1, amount - fixed)
        return jnp.zeros((amount,), jnp.int32).at[sequence[jnp.where(places < fixed, places, shifted)]].set(jnp.asarray(lengths, jnp.int32))

    lengths = jnp.where(number % 4 == 0, named(heavy_load, number // 4), named(common, number - number // 4 - 1))
    mixed = jax.random.permutation(jax.random.fold_in(own, 3), amount)
    giver, receiver = mixed[0:amount // 2 * 2:2], mixed[1:amount // 2 * 2:2]
    room = jnp.minimum(lengths[giver] - 1, limit - lengths[receiver]) // 2
    room = jnp.where((giver == sequence[0]) | (receiver == sequence[0]) | (lengths[receiver] == 0), 0, jnp.maximum(room, 0))
    shifted = jax.random.randint(jax.random.fold_in(own, 4), (amount // 2,), 0, 1 << 20) % (room + 1)
    lengths = lengths.at[giver].add(-shifted).at[receiver].add(shifted)
    members = jnp.searchsorted(jnp.cumsum(lengths), jnp.arange(rows * top), side="right").astype(jnp.int32)
    grid = members.reshape(top, rows).T
    grid = grid[jax.random.permutation(jax.random.fold_in(own, 1), rows)]
    turn = jax.random.randint(jax.random.fold_in(own, 2), (rows, 1), 0, top)
    return jnp.take_along_axis(grid, (jnp.arange(top)[None, :] + turn) % top, axis=1)


def load_shares(count, total, bound, skew, full):
    weights = [(1 << 20) // math.isqrt(grade ** skew) + 1 for grade in range(1, count + 1)]
    largest = bound if full else min(bound, max(-(-total // count), total * weights[0] // sum(weights)))
    least = 1 if total - largest >= count - 1 else 0
    counts, surplus = [largest] + [least] * (count - 1), total - largest - least * (count - 1)
    while surplus > 0:
        free = [i for i in range(1, count) if counts[i] < largest] or [i for i in range(1, count) if counts[i] < bound]
        mass, remaining = sum([weights[i] for i in free]), surplus
        for i in free:
            more = min(bound - counts[i], max(1, remaining * weights[i] // mass), surplus)
            counts[i] = counts[i] + more
            surplus = surplus - more
    return np.array(counts)


def scatter_about(own_key, dims, scale, reach, shards=(), held_as=jnp.bfloat16):
    entries = scale * jax.random.normal(own_key, dims, jnp.float32)
    if shards:
        entries = entries * shard_levels(own_key, dims, shards, -0.22, 0.18)
    return jnp.clip(entries, -reach, reach).astype(held_as)


def setup_inputs(seed: int = 0) -> dict:
    key_list = jax.random.split(jax.random.key(seed), 12)
    win_query = draw_win_query(jax.random.fold_in(key_list[11], 71), 0)
    win_key = draw_win_key(jax.random.fold_in(key_list[11], 71), 0)
    win_value = scatter_about(key_list[2], (BYTES, HEADS * HD), 1.0, 6.0, ((0, 32), (1, 8)))
    win_dout = scatter_about(key_list[3], (BYTES, HEADS * HD), 4.0, 16.0, ((0, 32), (1, 8)))
    cross_query = draw_cross_query(jax.random.fold_in(key_list[11], 71), 0)
    cross_dout = scatter_about(key_list[5], (BYTES, HEADS * HD), 4.0, 16.0, ((0, 32), (1, 8)))
    patch_key = draw_patch_key(jax.random.fold_in(key_list[11], 71), 0)
    patch_value = scatter_about(key_list[7], (PATCHES, HEADS * HD), 1.0, 6.0, ((0, 32), (1, 8)))
    patch_len = jax.vmap(lambda own: ragged(own, PB, BLK, LMAX, 2))(jax.random.split(key_list[8], BLOCKS)).reshape((BLOCKS, PB)).astype(jnp.int32)
    patch_owner_keys = jax.random.split(jax.random.fold_in(key_list[9], 1), PATCHES // (2 * PB))
    patch_owner_turns = jax.random.permutation(jax.random.fold_in(key_list[9], 3), PATCHES // (2 * PB))
    patch_owner = jax.vmap(lambda own, number: shared_out(jax.random.fold_in(key_list[9], 2), own, number, 2 * PB, N_SEQ, 1, CAP, 2))(patch_owner_keys, patch_owner_turns).reshape((PATCHES, 1))
    w_query = scatter_about(key_list[10], (D, HEADS * HD), (HEADS * HD) ** -0.5, 0.09375, ((0, 32), (1, 8)))
    return dict(win_query=win_query, win_key=win_key, win_value=win_value, win_dout=win_dout, cross_query=cross_query, cross_dout=cross_dout, patch_key=patch_key, patch_value=patch_value, patch_len=patch_len, patch_owner=patch_owner, w_query=w_query)


def row_stats(scores, allowed):
    masked = jnp.where(allowed, scores, -1e+30)
    row_top = lax.optimization_barrier(jnp.max(masked, axis=-1, keepdims=True))
    row_total = lax.optimization_barrier(jnp.sum(jnp.exp(jnp.where(allowed, scores - row_top, -1e+30)), axis=-1, keepdims=True))
    return row_top + jnp.log(row_total)

def window_block(query_block, dout_block, key_ext, value_ext, tail_valid):
    window = WIN
    inv_root = 1.0 / math.sqrt(HD)
    length = query_block.shape[0]
    width = query_block.shape[1]
    head_count = width // HD
    query_heads = query_block.astype(jnp.float32).reshape(length, head_count, HD)
    dout_heads = dout_block.astype(jnp.float32).reshape(length, head_count, HD)
    key_heads = key_ext.astype(jnp.float32).reshape(length + window, head_count, HD)
    value_heads = value_ext.astype(jnp.float32).reshape(length + window, head_count, HD)
    rows_at = lax.broadcasted_iota(jnp.int32, (window, 2 * window), 0)
    cols_at = lax.broadcasted_iota(jnp.int32, (window, 2 * window), 1)
    gap = cols_at - rows_at

    def one_step(sub_step, state_in):
        dq_acc, dk_acc, dv_acc = state_in
        offset = sub_step * window
        query_sub = lax.dynamic_slice_in_dim(query_heads, offset, window, 0)
        dout_sub = lax.dynamic_slice_in_dim(dout_heads, offset, window, 0)
        key_sub = lax.dynamic_slice_in_dim(key_heads, offset, 2 * window, 0)
        value_sub = lax.dynamic_slice_in_dim(value_heads, offset, 2 * window, 0)
        allowed = ((gap >= 0) & (gap <= window) & ((cols_at + offset >= window) | tail_valid))[None]
        scores = jnp.einsum('qhd,khd->hqk', query_sub, key_sub) * inv_root
        log_total = row_stats(scores, allowed)
        prob_rows = jnp.exp(jnp.where(allowed, scores - log_total, -1e+30))
        dprobs = jnp.einsum('qhd,khd->hqk', dout_sub, value_sub)
        row_delta = lax.optimization_barrier(jnp.sum(prob_rows * dprobs, axis=-1, keepdims=True))
        grad_low = lax.optimization_barrier((prob_rows * (dprobs - row_delta) * inv_root).astype(jnp.bfloat16))
        probs_low = lax.optimization_barrier(prob_rows.astype(jnp.bfloat16))
        grad_wide = grad_low.astype(jnp.float32)
        probs_wide = probs_low.astype(jnp.float32)
        dq_sub = jnp.einsum('hqk,khd->qhd', grad_wide, key_sub)
        dk_sub = jnp.einsum('hqk,qhd->khd', grad_wide, query_sub)
        dv_sub = jnp.einsum('hqk,qhd->khd', probs_wide, dout_sub)
        dq_acc = lax.dynamic_update_slice_in_dim(dq_acc, dq_sub, offset, 0)
        dk_acc = lax.dynamic_update_slice_in_dim(dk_acc, lax.dynamic_slice_in_dim(dk_acc, offset, 2 * window, 0) + dk_sub, offset, 0)
        dv_acc = lax.dynamic_update_slice_in_dim(dv_acc, lax.dynamic_slice_in_dim(dv_acc, offset, 2 * window, 0) + dv_sub, offset, 0)
        return (dq_acc, dk_acc, dv_acc)
    start_state = (jnp.zeros((length, head_count, HD), jnp.float32), jnp.zeros((length + window, head_count, HD), jnp.float32), jnp.zeros((length + window, head_count, HD), jnp.float32))
    dq_acc, dk_acc, dv_acc = lax.fori_loop(0, length // window, one_step, start_state)
    return (dq_acc.reshape(length, width), dk_acc.reshape(length + window, width), dv_acc.reshape(length + window, width))

def cross_block(items):
    query_block, dout_block, key_rows, value_rows, length_row = items
    inv_root = 1.0 / math.sqrt(HD)
    width = query_block.shape[1]
    head_count = width // HD
    query_heads = query_block.astype(jnp.float32).reshape(BLK, head_count, HD)
    dout_heads = dout_block.astype(jnp.float32).reshape(BLK, head_count, HD)
    key_heads = key_rows.astype(jnp.float32).reshape(PB, head_count, HD)
    value_heads = value_rows.astype(jnp.float32).reshape(PB, head_count, HD)
    starts = jnp.cumsum(length_row) - length_row
    within = jnp.arange(BLK)
    allowed = (starts[None, :] <= within[:, None])[None]
    scores = jnp.einsum('qhd,khd->hqk', query_heads, key_heads) * inv_root
    log_total = row_stats(scores, allowed)
    prob_rows = jnp.exp(jnp.where(allowed, scores - log_total, -1e+30))
    dprobs = jnp.einsum('qhd,khd->hqk', dout_heads, value_heads)
    row_delta = lax.optimization_barrier(jnp.sum(prob_rows * dprobs, axis=-1, keepdims=True))
    grad_low = lax.optimization_barrier((prob_rows * (dprobs - row_delta) * inv_root).astype(jnp.bfloat16))
    probs_low = lax.optimization_barrier(prob_rows.astype(jnp.bfloat16))
    grad_wide = grad_low.astype(jnp.float32)
    probs_wide = probs_low.astype(jnp.float32)
    dq_rows = jnp.einsum('hqk,khd->qhd', grad_wide, key_heads).reshape(BLK, width).astype(jnp.bfloat16)
    dk_rows = jnp.einsum('hqk,qhd->khd', grad_wide, query_heads).reshape(PB, width).astype(jnp.bfloat16)
    dv_rows = jnp.einsum('hqk,qhd->khd', probs_wide, dout_heads).reshape(PB, width).astype(jnp.bfloat16)
    return (dq_rows, dk_rows, dv_rows)

def reference(win_query, win_key, win_value, win_dout, cross_query, cross_dout, patch_key, patch_value, patch_len, patch_owner, w_query):
    width = HEADS * HD
    seq_of_stored = np.array([row_block // 2 if row_block % 2 == 0 else BLOCKS - 1 - row_block // 2 for row_block in range(BLOCKS)])
    stored_of_seq = np.argsort(seq_of_stored)

    def to_seq(values):
        return values.reshape(BLOCKS, BLK, width)[stored_of_seq]

    def to_stored(values):
        return values[seq_of_stored].reshape(BYTES, width)
    query_seq = to_seq(win_query)
    dout_seq = to_seq(win_dout)
    key_seq = to_seq(win_key)
    value_seq = to_seq(win_value)
    zero_rim = jnp.zeros((1, WIN, width), win_key.dtype)
    key_rims = jnp.concatenate([zero_rim, key_seq[:-1, BLK - WIN:]], axis=0)
    value_rims = jnp.concatenate([zero_rim, value_seq[:-1, BLK - WIN:]], axis=0)
    rim_valid = jnp.arange(BLOCKS) > 0

    def one_block(items):
        query_block, dout_block, key_block, value_block, key_rim, value_rim, valid = items
        return window_block(query_block, dout_block, jnp.concatenate([key_rim, key_block], axis=0), jnp.concatenate([value_rim, value_block], axis=0), valid)
    dq_seq, dk_ext, dv_ext = lax.map(one_block, (query_seq, dout_seq, key_seq, value_seq, key_rims, value_rims, rim_valid))
    dk_seq = dk_ext[:, WIN:].at[:-1, BLK - WIN:].add(dk_ext[1:, :WIN])
    dv_seq = dv_ext[:, WIN:].at[:-1, BLK - WIN:].add(dv_ext[1:, :WIN])
    win_dq = to_stored(dq_seq.astype(jnp.bfloat16))
    win_dk = to_stored(dk_seq.astype(jnp.bfloat16))
    win_dv = to_stored(dv_seq.astype(jnp.bfloat16))
    cross_items = (cross_query.reshape(BLOCKS, BLK, width), cross_dout.reshape(BLOCKS, BLK, width), patch_key.reshape(BLOCKS, PB, width), patch_value.reshape(BLOCKS, PB, width), patch_len)
    dq_blocks, dk_blocks, dv_blocks = lax.map(cross_block, cross_items)
    cross_dq = dq_blocks.reshape(BYTES, width)
    patch_dk = dk_blocks.reshape(PATCHES, width)
    patch_dv = dv_blocks.reshape(PATCHES, width)
    owners = patch_owner[:, 0].reshape(N_SEQ, 2 * PB).astype(jnp.int32)
    onehot = (owners[:, :, None] == jnp.arange(N_SEQ).astype(jnp.int32)[None, None, :]).astype(jnp.int32)
    slot_rank = lax.optimization_barrier(jnp.sum(onehot * (jnp.cumsum(onehot, axis=1) - onehot), axis=2))
    slot_index = (owners * CAP + slot_rank).astype(jnp.int32)
    stacked = jnp.stack([patch_dk, patch_dv]).reshape(2, N_SEQ, 2 * PB, width)
    sources = jnp.arange(N_SEQ).astype(jnp.int32)[:, None]
    placed = jnp.zeros((2, N_SEQ, N_SEQ * CAP, width), jnp.bfloat16).at[:, sources, slot_index].set(stacked)
    patch_grads = placed.reshape(2, N_SEQ, N_SEQ, CAP, width).transpose(0, 2, 1, 3, 4).reshape(2, SLOTS, width)
    group_cols = width // N_MP

    def add_group(group, accum):
        begin = group * group_cols
        dq_group = lax.dynamic_slice_in_dim(cross_dq, begin, group_cols, 1)
        w_group = lax.dynamic_slice_in_dim(w_query, begin, group_cols, 1)
        part_low = lax.optimization_barrier(jnp.dot(dq_group, w_group.T, preferred_element_type=jnp.float32).astype(jnp.bfloat16))
        return accum + part_low.astype(jnp.float32)
    byte_sum = lax.fori_loop(0, N_MP, add_group, jnp.zeros((BYTES, D), jnp.float32))
    byte_grads = byte_sum.astype(jnp.bfloat16)
    return (win_dq, win_dk, win_dv, patch_grads, byte_grads)
```

```python
import functools
import math

import jax
import jax.numpy as jnp
from jax import lax
from jax.experimental import pallas as pl
from jax.experimental.pallas import tpu as pltpu
from jax.sharding import PartitionSpec as P

HD = 128
WIN = 256
INV_ROOT = 1.0 / math.sqrt(HD)
F32 = jnp.float32
BF16 = jnp.bfloat16


def dot(a, b, ca, cb):
    return lax.dot_general(a, b, (((ca,), (cb,)), ((), ())), preferred_element_type=F32)


def window_block(q, do, k_rim, v_rim, k_own, v_own, rim_ok, own_ok):
    s_rim = jnp.where(rim_ok, dot(k_rim, q, 1, 1), -1e30)
    s_own = jnp.where(own_ok, dot(k_own, q, 1, 1), -1e30)
    top = jnp.maximum(
        jnp.max(s_rim, axis=0, keepdims=True), jnp.max(s_own, axis=0, keepdims=True)
    )
    e_rim = jnp.exp((s_rim - top) * INV_ROOT)
    e_own = jnp.exp((s_own - top) * INV_ROOT)
    scale = 1.0 / (
        jnp.sum(e_rim, axis=0, keepdims=True) + jnp.sum(e_own, axis=0, keepdims=True)
    )
    d_rim = dot(v_rim, do, 1, 1)
    d_own = dot(v_own, do, 1, 1)
    p_rim = e_rim * scale
    p_own = e_own * scale
    delta = jnp.sum(p_rim * d_rim, axis=0, keepdims=True) + jnp.sum(
        p_own * d_own, axis=0, keepdims=True
    )
    g_rim = (p_rim * (d_rim - delta) * INV_ROOT).astype(BF16)
    g_own = (p_own * (d_own - delta) * INV_ROOT).astype(BF16)
    p_rim = p_rim.astype(BF16)
    p_own = p_own.astype(BF16)
    dq = dot(g_rim, k_rim, 0, 0) + dot(g_own, k_own, 0, 0)
    return (
        dq,
        dot(g_rim, q, 1, 0),
        dot(p_rim, do, 1, 0),
        dot(g_own, q, 1, 0),
        dot(p_own, do, 1, 0),
    )


def window_kernel(
    flags, q_ref, do_ref, k_ref, v_ref, before_ref, after_ref,
    dq_ref, dk_ref, dv_ref, low_ref, high_ref,
):
    low_valid = flags[0]
    is_last = flags[1]
    rows = lax.broadcasted_iota(jnp.int32, (WIN, WIN), 0)
    cols = lax.broadcasted_iota(jnp.int32, (WIN, WIN), 1)
    rim_ok = rows >= cols
    own_ok = rows <= cols
    lo = slice(0, WIN)
    hi = slice(WIN, 2 * WIN)
    k_low, v_low = k_ref[lo, :], v_ref[lo, :]
    dq, dk_r, dv_r, dk_low, dv_low = window_block(
        q_ref[lo, :], do_ref[lo, :], before_ref[0], before_ref[1], k_low, v_low,
        rim_ok & (low_valid > 0), own_ok,
    )
    dq_ref[lo, :] = dq.astype(BF16)
    low_ref[0] = dk_r.astype(BF16)
    low_ref[1] = dv_r.astype(BF16)
    last = is_last > 0
    k_prev = jnp.where(last, k_low, after_ref[0])
    v_prev = jnp.where(last, v_low, after_ref[1])
    dq, dk_r, dv_r, dk_own, dv_own = window_block(
        q_ref[hi, :], do_ref[hi, :], k_prev, v_prev, k_ref[hi, :], v_ref[hi, :],
        rim_ok, own_ok,
    )
    dq_ref[hi, :] = dq.astype(BF16)
    high_ref[0] = dk_r.astype(BF16)
    high_ref[1] = dv_r.astype(BF16)
    dk_ref[hi, :] = dk_own
    dv_ref[hi, :] = dv_own
    dk_ref[lo, :] = dk_low + jnp.where(last, dk_r, 0.0)
    dv_ref[lo, :] = dv_low + jnp.where(last, dv_r, 0.0)


def window_call(flags, q, do, k, v, before, after):
    rows, width = q.shape
    full = pl.BlockSpec((rows, HD), lambda h, f: (0, h))
    rim = pl.BlockSpec((2, WIN, HD), lambda h, f: (0, 0, h))
    return pl.pallas_call(
        window_kernel,
        grid_spec=pltpu.PrefetchScalarGridSpec(
            num_scalar_prefetch=1,
            grid=(width // HD,),
            in_specs=[full] * 4 + [rim] * 2,
            out_specs=[full, full, full, rim, rim],
        ),
        out_shape=(
            jax.ShapeDtypeStruct((rows, width), BF16),
            jax.ShapeDtypeStruct((rows, width), F32),
            jax.ShapeDtypeStruct((rows, width), F32),
            jax.ShapeDtypeStruct((2, WIN, width), BF16),
            jax.ShapeDtypeStruct((2, WIN, width), BF16),
        ),
        name="window_grads",
        compiler_params=pltpu.CompilerParams(vmem_limit_bytes=40 << 20),
    )(flags, q, do, k, v, before, after)


def cross_kernel(q_ref, do_ref, k_ref, v_ref, len_ref, owner_ref, dq_ref, buf_ref, sel_ref):
    blocks = len_ref.shape[0]
    per_block = len_ref.shape[1]
    rows = q_ref.shape[0] // blocks
    patches = blocks * per_block
    slots = sel_ref.shape[0]
    cap = buf_ref.shape[2]

    @pl.when(pl.program_id(0) == 0)
    def _():
        owner_col = jnp.broadcast_to(owner_ref[...], (patches, patches))
        owner_row = owner_col.T
        earlier = lax.broadcasted_iota(
            jnp.int32, (patches, patches), 0
        ) < lax.broadcasted_iota(jnp.int32, (patches, patches), 1)
        same = jnp.where((owner_col == owner_row) & earlier, 1, 0)
        rank = jnp.sum(same, axis=0, keepdims=True)
        slot = owner_ref[...] * cap + rank
        at = lax.broadcasted_iota(jnp.int32, (slots, patches), 0)
        sel_ref[...] = jnp.where(at == slot, 1.0, 0.0).astype(BF16)

    before = lax.broadcasted_iota(
        jnp.int32, (per_block, per_block), 1
    ) < lax.broadcasted_iota(jnp.int32, (per_block, per_block), 0)
    starts = dot(
        jnp.where(before, 1.0, 0.0).astype(BF16), len_ref[...].astype(F32).astype(BF16), 1, 1
    ).astype(jnp.int32)
    within = lax.broadcasted_iota(jnp.int32, (per_block, rows), 1)
    dks, dvs = [], []
    for b in range(blocks):
        r = slice(b * rows, (b + 1) * rows)
        p = slice(b * per_block, (b + 1) * per_block)
        q, do, k, v = q_ref[r, :], do_ref[r, :], k_ref[p, :], v_ref[p, :]
        ok = starts[:, b : b + 1] <= within
        s = jnp.where(ok, dot(k, q, 1, 1), -1e30)
        e = jnp.exp((s - jnp.max(s, axis=0, keepdims=True)) * INV_ROOT)
        probs = e * (1.0 / jnp.sum(e, axis=0, keepdims=True))
        d = dot(v, do, 1, 1)
        delta = jnp.sum(probs * d, axis=0, keepdims=True)
        g = (probs * (d - delta) * INV_ROOT).astype(BF16)
        dq_ref[r, :] = dot(g, k, 0, 0).astype(BF16)
        dks.append(dot(g, q, 1, 0).astype(BF16))
        dvs.append(dot(probs.astype(BF16), do, 1, 0).astype(BF16))
    sel = sel_ref[...]
    for i, parts in enumerate((dks, dvs)):
        placed = dot(sel, jnp.concatenate(parts, axis=0), 1, 0).astype(BF16)
        buf_ref[:, i] = placed.reshape(slots // cap, cap, HD)


def cross_call(q, do, k, v, lens, owners, owner_count):
    rows, width = q.shape
    patches = k.shape[0]
    cap = max(2, 2 * (patches // owner_count))
    col = pl.BlockSpec((rows, HD), lambda h: (0, h))
    pcol = pl.BlockSpec((patches, HD), lambda h: (0, h))
    return pl.pallas_call(
        cross_kernel,
        grid_spec=pltpu.PrefetchScalarGridSpec(
            num_scalar_prefetch=0,
            grid=(width // HD,),
            in_specs=[
                col, col, pcol, pcol,
                pl.BlockSpec(lens.shape, lambda h: (0, 0)),
                pl.BlockSpec((1, patches), lambda h: (0, 0)),
            ],
            out_specs=[
                col,
                pl.BlockSpec((owner_count, 2, cap, HD), lambda h: (0, 0, 0, h)),
            ],
            scratch_shapes=[pltpu.VMEM((owner_count * cap, patches), BF16)],
        ),
        out_shape=(
            jax.ShapeDtypeStruct((rows, width), BF16),
            jax.ShapeDtypeStruct((owner_count, 2, cap, width), BF16),
        ),
        name="cross_grads",
        compiler_params=pltpu.CompilerParams(vmem_limit_bytes=40 << 20),
    )(q, do, k, v, lens, owners.reshape(1, patches))


def join_kernel(dk_ref, dv_ref, low_ref, high_ref, dk_out, dv_out):
    for i, (src, out) in enumerate(((dk_ref, dk_out), (dv_ref, dv_out))):
        out[:WIN, :] = (src[:WIN, :] + low_ref[i].astype(F32)).astype(BF16)
        out[WIN:, :] = (src[WIN:, :] + high_ref[i].astype(F32)).astype(BF16)


def join_call(dk, dv, low_back, high_back):
    rows, width = dk.shape
    step = 2 * HD
    col = pl.BlockSpec((rows, step), lambda h: (0, h))
    rim = pl.BlockSpec((2, WIN, step), lambda h: (0, 0, h))
    out = jax.ShapeDtypeStruct((rows, width), BF16)
    return pl.pallas_call(
        join_kernel,
        grid=(width // step,),
        in_specs=[col, col, rim, rim],
        out_specs=[col, col],
        out_shape=(out, out),
        name="join_rims",
        compiler_params=pltpu.CompilerParams(vmem_limit_bytes=40 << 20),
    )(dk, dv, low_back, high_back)


def shifted(block, axis, distance):
    devices = range(lax.axis_size(axis))
    route = [(i - distance, i) for i in devices if i - distance in devices]
    return lax.ppermute(block, axis, route)


def local(
    win_query, win_key, win_value, win_dout, cross_query, cross_dout,
    patch_key, patch_value, patch_len, patch_owner, w_query,
):
    seq_count = lax.axis_size("seq")
    seq_index = lax.axis_index("seq")
    flags = jnp.stack([seq_index > 0, seq_index == seq_count - 1]).astype(jnp.int32)
    low_rim = jnp.stack([win_key[:WIN], win_value[:WIN]])
    high_rim = jnp.stack([win_key[WIN:], win_value[WIN:]])
    before = shifted(low_rim, "seq", 1)
    after = shifted(high_rim, "seq", -1)
    cross_dq, buffer = cross_call(
        cross_query, cross_dout, patch_key, patch_value, patch_len, patch_owner, seq_count
    )
    win_dq, dk, dv, low_send, high_send = window_call(
        flags, win_query, win_dout, win_key, win_value, before, after
    )
    low_back = shifted(low_send, "seq", -1)
    high_back = shifted(high_send, "seq", 1)
    win_dk, win_dv = join_call(dk, dv, low_back, high_back)
    arrived = lax.all_to_all(buffer, "seq", split_axis=0, concat_axis=0, tiled=True)
    patch_grads = arrived.transpose(1, 0, 2, 3).reshape(2, -1, arrived.shape[3])
    partial_sums = lax.dot_general(
        cross_dq,
        lax.all_gather(w_query, "seq", axis=0, tiled=True),
        (((1,), (1,)), ((), ())),
        preferred_element_type=F32,
    )
    byte_grads = lax.psum_scatter(
        partial_sums.astype(BF16), "mp", scatter_dimension=1, tiled=True
    )
    return (win_dq, win_dk, win_dv, patch_grads, byte_grads)


def solution(mesh):
    tile = P("seq", "mp")
    rows = P("seq", None)
    in_specs = (tile,) * 8 + (rows, rows, tile)
    out_specs = (tile, tile, tile, P(None, "seq", "mp"), tile)
    return jax.shard_map(local, mesh=mesh, in_specs=in_specs, out_specs=out_specs, check_vma=False)
```

```python
import functools
import math

import jax
import jax.numpy as jnp
from jax import lax
from jax.experimental import pallas as pl
from jax.experimental.pallas import tpu as pltpu
from jax.sharding import PartitionSpec as P

HD = 128
WIN = 256
INV_ROOT = 1.0 / math.sqrt(HD)
F32 = jnp.float32
BF16 = jnp.bfloat16


def dot(a, b, ca, cb):
    return lax.dot_general(a, b, (((ca,), (cb,)), ((), ())), preferred_element_type=F32)


def window_block(q, do, k_rim, v_rim, k_own, v_own, rim_ok, own_ok):
    s_rim = jnp.where(rim_ok, dot(k_rim, q, 1, 1), -1e30)
    s_own = jnp.where(own_ok, dot(k_own, q, 1, 1), -1e30)
    top = jnp.maximum(
        jnp.max(s_rim, axis=0, keepdims=True), jnp.max(s_own, axis=0, keepdims=True)
    )
    e_rim = jnp.exp((s_rim - top) * INV_ROOT)
    e_own = jnp.exp((s_own - top) * INV_ROOT)
    scale = 1.0 / (
        jnp.sum(e_rim, axis=0, keepdims=True) + jnp.sum(e_own, axis=0, keepdims=True)
    )
    d_rim = dot(v_rim, do, 1, 1)
    d_own = dot(v_own, do, 1, 1)
    p_rim = e_rim * scale
    p_own = e_own * scale
    delta = jnp.sum(p_rim * d_rim, axis=0, keepdims=True) + jnp.sum(
        p_own * d_own, axis=0, keepdims=True
    )
    g_rim = (p_rim * (d_rim - delta) * INV_ROOT).astype(BF16)
    g_own = (p_own * (d_own - delta) * INV_ROOT).astype(BF16)
    p_rim = p_rim.astype(BF16)
    p_own = p_own.astype(BF16)
    dq = dot(g_rim, k_rim, 0, 0) + dot(g_own, k_own, 0, 0)
    return (
        dq,
        dot(g_rim, q, 1, 0),
        dot(p_rim, do, 1, 0),
        dot(g_own, q, 1, 0),
        dot(p_own, do, 1, 0),
    )


def window_kernel(
    flags, q_ref, do_ref, k_ref, v_ref, before_ref, after_ref,
    dq_ref, dk_ref, dv_ref, low_ref, high_ref,
):
    low_valid = flags[0]
    is_last = flags[1]
    rows = lax.broadcasted_iota(jnp.int32, (WIN, WIN), 0)
    cols = lax.broadcasted_iota(jnp.int32, (WIN, WIN), 1)
    rim_ok = rows >= cols
    own_ok = rows <= cols
    lo = slice(0, WIN)
    hi = slice(WIN, 2 * WIN)
    k_low, v_low = k_ref[lo, :], v_ref[lo, :]
    dq, dk_r, dv_r, dk_low, dv_low = window_block(
        q_ref[lo, :], do_ref[lo, :], before_ref[0], before_ref[1], k_low, v_low,
        rim_ok & (low_valid > 0), own_ok,
    )
    dq_ref[lo, :] = dq.astype(BF16)
    low_ref[0] = dk_r.astype(BF16)
    low_ref[1] = dv_r.astype(BF16)
    last = is_last > 0
    k_prev = jnp.where(last, k_low, after_ref[0])
    v_prev = jnp.where(last, v_low, after_ref[1])
    dq, dk_r, dv_r, dk_own, dv_own = window_block(
        q_ref[hi, :], do_ref[hi, :], k_prev, v_prev, k_ref[hi, :], v_ref[hi, :],
        rim_ok, own_ok,
    )
    dq_ref[hi, :] = dq.astype(BF16)
    high_ref[0] = dk_r.astype(BF16)
    high_ref[1] = dv_r.astype(BF16)
    dk_ref[hi, :] = dk_own
    dv_ref[hi, :] = dv_own
    dk_ref[lo, :] = dk_low + jnp.where(last, dk_r, 0.0)
    dv_ref[lo, :] = dv_low + jnp.where(last, dv_r, 0.0)


def window_call(flags, q, do, k, v, before, after):
    rows, width = q.shape
    full = pl.BlockSpec((rows, HD), lambda h, f: (0, h))
    rim = pl.BlockSpec((2, WIN, HD), lambda h, f: (0, 0, h))
    return pl.pallas_call(
        window_kernel,
        grid_spec=pltpu.PrefetchScalarGridSpec(
            num_scalar_prefetch=1,
            grid=(width // HD,),
            in_specs=[full] * 4 + [rim] * 2,
            out_specs=[full, full, full, rim, rim],
        ),
        out_shape=(
            jax.ShapeDtypeStruct((rows, width), BF16),
            jax.ShapeDtypeStruct((rows, width), F32),
            jax.ShapeDtypeStruct((rows, width), F32),
            jax.ShapeDtypeStruct((2, WIN, width), BF16),
            jax.ShapeDtypeStruct((2, WIN, width), BF16),
        ),
        name="window_grads",
        compiler_params=pltpu.CompilerParams(vmem_limit_bytes=40 << 20),
    )(flags, q, do, k, v, before, after)


def cross_kernel(q_ref, do_ref, k_ref, v_ref, len_ref, owner_ref, dq_ref, buf_ref, sel_ref):
    blocks = len_ref.shape[0]
    per_block = len_ref.shape[1]
    rows = q_ref.shape[0] // blocks
    patches = blocks * per_block
    slots = sel_ref.shape[0]
    cap = buf_ref.shape[2]

    @pl.when(pl.program_id(0) == 0)
    def _():
        owner_col = jnp.broadcast_to(owner_ref[...], (patches, patches))
        owner_row = owner_col.T
        earlier = lax.broadcasted_iota(
            jnp.int32, (patches, patches), 0
        ) < lax.broadcasted_iota(jnp.int32, (patches, patches), 1)
        same = jnp.where((owner_col == owner_row) & earlier, 1, 0)
        rank = jnp.sum(same, axis=0, keepdims=True)
        slot = owner_ref[...] * cap + rank
        at = lax.broadcasted_iota(jnp.int32, (slots, patches), 0)
        sel_ref[...] = jnp.where(at == slot, 1.0, 0.0).astype(BF16)

    before = lax.broadcasted_iota(
        jnp.int32, (per_block, per_block), 1
    ) < lax.broadcasted_iota(jnp.int32, (per_block, per_block), 0)
    starts = dot(
        jnp.where(before, 1.0, 0.0).astype(BF16), len_ref[...].astype(F32).astype(BF16), 1, 1
    ).astype(jnp.int32)
    within = lax.broadcasted_iota(jnp.int32, (per_block, rows), 1)
    dks, dvs = [], []
    for b in range(blocks):
        r = slice(b * rows, (b + 1) * rows)
        p = slice(b * per_block, (b + 1) * per_block)
        q, do, k, v = q_ref[r, :], do_ref[r, :], k_ref[p, :], v_ref[p, :]
        ok = starts[:, b : b + 1] <= within
        s = jnp.where(ok, dot(k, q, 1, 1), -1e30)
        e = jnp.exp((s - jnp.max(s, axis=0, keepdims=True)) * INV_ROOT)
        probs = e * (1.0 / jnp.sum(e, axis=0, keepdims=True))
        d = dot(v, do, 1, 1)
        delta = jnp.sum(probs * d, axis=0, keepdims=True)
        g = (probs * (d - delta) * INV_ROOT).astype(BF16)
        dq_ref[r, :] = dot(g, k, 0, 0).astype(BF16)
        dks.append(dot(g, q, 1, 0).astype(BF16))
        dvs.append(dot(probs.astype(BF16), do, 1, 0).astype(BF16))
    sel = sel_ref[...]
    for i, parts in enumerate((dks, dvs)):
        placed = dot(sel, jnp.concatenate(parts, axis=0), 1, 0).astype(BF16)
        buf_ref[:, i] = placed.reshape(slots // cap, cap, HD)


def cross_call(q, do, k, v, lens, owners, owner_count):
    rows, width = q.shape
    patches = k.shape[0]
    cap = max(2, 2 * (patches // owner_count))
    col = pl.BlockSpec((rows, HD), lambda h: (0, h))
    pcol = pl.BlockSpec((patches, HD), lambda h: (0, h))
    return pl.pallas_call(
        cross_kernel,
        grid_spec=pltpu.PrefetchScalarGridSpec(
            num_scalar_prefetch=0,
            grid=(width // HD,),
            in_specs=[
                col, col, pcol, pcol,
                pl.BlockSpec(lens.shape, lambda h: (0, 0)),
                pl.BlockSpec((1, patches), lambda h: (0, 0)),
            ],
            out_specs=[
                col,
                pl.BlockSpec((owner_count, 2, cap, HD), lambda h: (0, 0, 0, h)),
            ],
            scratch_shapes=[pltpu.VMEM((owner_count * cap, patches), BF16)],
        ),
        out_shape=(
            jax.ShapeDtypeStruct((rows, width), BF16),
            jax.ShapeDtypeStruct((owner_count, 2, cap, width), BF16),
        ),
        name="cross_grads",
        compiler_params=pltpu.CompilerParams(vmem_limit_bytes=40 << 20),
    )(q, do, k, v, lens, owners.reshape(1, patches))


def join_kernel(dk_ref, dv_ref, low_ref, high_ref, dk_out, dv_out):
    for i, (src, out) in enumerate(((dk_ref, dk_out), (dv_ref, dv_out))):
        out[:WIN, :] = (src[:WIN, :] + low_ref[i].astype(F32)).astype(BF16)
        out[WIN:, :] = (src[WIN:, :] + high_ref[i].astype(F32)).astype(BF16)


def join_call(dk, dv, low_back, high_back):
    rows, width = dk.shape
    step = 2 * HD
    col = pl.BlockSpec((rows, step), lambda h: (0, h))
    rim = pl.BlockSpec((2, WIN, step), lambda h: (0, 0, h))
    out = jax.ShapeDtypeStruct((rows, width), BF16)
    return pl.pallas_call(
        join_kernel,
        grid=(width // step,),
        in_specs=[col, col, rim, rim],
        out_specs=[col, col],
        out_shape=(out, out),
        name="join_rims",
        compiler_params=pltpu.CompilerParams(vmem_limit_bytes=40 << 20),
    )(dk, dv, low_back, high_back)


def shifted(block, axis, distance):
    devices = range(lax.axis_size(axis))
    route = [(i - distance, i) for i in devices if i - distance in devices]
    return lax.ppermute(block, axis, route)


NZ, NX, NY, NC = 8, 4, 4, 2


def place(z, x, y, c):
    return ((z % NZ) * NX + x % NX) * (NY * NC) + (y % NY) * NC + c


def send(block, target):
    route = []
    for z in range(NZ):
        for x in range(NX):
            for y in range(NY):
                for c in range(NC):
                    to = target(z, x, y, c)
                    if to is not None:
                        route.append((place(z, x, y, c), place(*to)))
    return lax.ppermute(block, ("seq", "mp"), route)


def two(zs, xs):
    def target(z, x, y, c):
        if c == 0:
            return None if zs is None else (z + zs, x, y, c)
        return None if xs is None else (z, x + xs, y, c)

    return target


def cross_two(xs, zs):
    def target(z, x, y, c):
        if c == 0:
            return None if xs is None else (z, x + xs, y, c)
        return None if zs is None else (z + zs, x, y, c)

    return target


SUB = (0, -1, 1, -2)
FAR = (2, -3, 3, -4)


def gather_weight(w_rows, first_core):
    own = send(w_rows, lambda z, x, y, c: (z + NC * y + c, x, z // NC, z % NC))
    a1 = send(own, cross_two(1, 1))
    a2 = send(own, cross_two(-1, -1))
    a3 = send(own, cross_two(2, 2))
    a4 = send(own, cross_two(None, -2))
    a5 = send(a3, cross_two(None, 1))
    a6 = send(a4, cross_two(None, -1))
    a7 = send(own, cross_two(None, 4))
    near = jnp.concatenate([own, a1, a2, a3], axis=0)
    far = jnp.concatenate([a4, a5, a6, a7], axis=0)
    b1 = send(near, two(1, 1))
    b2 = send(near, two(-1, -1))
    b3 = send(near, two(2, 2))
    b4 = send(jnp.where(first_core, near, far), two(-2, 1))
    b5 = send(jnp.where(first_core, b3, far), two(1, -1))
    b6 = send(jnp.where(first_core, b4, far), two(-1, 2))
    half = near.shape[0] // 2
    b7 = send(b3[:half], two(2, None))
    b8 = send(b4[half:], two(-2, None))
    return [near, b1, b2, b3, b4, b5, b6], far, b7, b8


def gather_rows(dq):
    swap = lambda z, x, y, c: (z, x, y, 1 - c)
    parts = [dq]
    for dy in (1, -1, 2):
        parts.append(send(dq, lambda z, x, y, c, dy=dy: (z, x, y + dy, c)))
    return parts + [send(p, swap) for p in parts]


def product_kernel(pos, *refs):
    rows = refs[:8]
    near = refs[8:15]
    far, b7, b8, out_ref, a_buf, w_buf, a_sem, w_sem = refs[15:]
    z, x, m, c = pos[0], pos[1], pos[2], pos[3]
    y = m // NC
    shard = w_buf.shape[1] // NX
    half = shard * NX // 2

    def copy_w(src, row, dz, dx):
        k = lax.rem(z + dz - m + 2 * NZ, NZ)
        n = lax.rem(x + dx + NX, NX)
        return pltpu.make_async_copy(
            src.at[pl.ds(row, shard), :],
            w_buf.at[k, pl.ds(pl.multiple_of(n * shard, shard), shard), :],
            w_sem.at[k * NX + n],
        )

    for i, src in enumerate(rows):
        dy = (0, -1, 1, 2)[i % 4]
        other = c if i < 4 else 1 - c
        k = NC * lax.rem(y + dy + NY, NY) + other
        pltpu.make_async_copy(src, a_buf.at[k], a_sem.at[k]).start()

    @pl.when(c == 0)
    def _():
        for src, dz in zip(near, (0, -1, 1, -2, 2, -3, 3)):
            for i, dx in enumerate(SUB):
                copy_w(src, i * shard, dz, dx).start()
        for i, dx in enumerate(SUB):
            src = b7 if i < 2 else b8
            copy_w(src, (i % 2) * shard, -4, dx).start()

    @pl.when(c != 0)
    def _():
        for src, dx, offs in zip(
            near + (far,),
            (0, -1, 1, -2, -1, 1, -2, 0),
            (SUB, SUB, SUB, SUB, FAR, FAR, FAR, FAR),
        ):
            for i, dz in enumerate(offs):
                copy_w(src, i * shard, dz, dx).start()

    total = None
    for k in range(NZ):
        pltpu.make_async_copy(rows[0], a_buf.at[k], a_sem.at[k]).wait()
        for n in range(NX):
            pltpu.make_async_copy(
                near[0].at[pl.ds(0, shard), :],
                w_buf.at[k, pl.ds(n * shard, shard), :],
                w_sem.at[k * NX + n],
            ).wait()
        part = dot(a_buf[k], w_buf[k], 1, 1)
        total = part if total is None else total + part
    out_ref[...] = total.astype(BF16)


def product_call(pos, rows, near, far, b7, b8):
    count, width = rows[0].shape
    n_rows = near[0].shape[0]
    anywhere = pl.BlockSpec(memory_space=pl.ANY)
    return pl.pallas_call(
        product_kernel,
        grid_spec=pltpu.PrefetchScalarGridSpec(
            num_scalar_prefetch=1,
            grid=(1,),
            in_specs=[anywhere] * 18,
            out_specs=pl.BlockSpec((count, n_rows), lambda i, p: (0, 0)),
            scratch_shapes=[
                pltpu.VMEM((NZ, count, width), BF16),
                pltpu.VMEM((NZ, n_rows, width), BF16),
                pltpu.SemaphoreType.DMA((NZ,)),
                pltpu.SemaphoreType.DMA((NZ * NX,)),
            ],
        ),
        out_shape=jax.ShapeDtypeStruct((count, n_rows), BF16),
        name="byte_product",
        compiler_params=pltpu.CompilerParams(vmem_limit_bytes=40 << 20),
    )(pos, *rows, *near, far, b7, b8)


def local(
    win_query, win_key, win_value, win_dout, cross_query, cross_dout,
    patch_key, patch_value, patch_len, patch_owner, w_query,
):
    seq_count = lax.axis_size("seq")
    seq_index = lax.axis_index("seq")
    mp_index = lax.axis_index("mp")
    flags = jnp.stack([seq_index > 0, seq_index == seq_count - 1]).astype(jnp.int32)
    core = mp_index % NC
    pos = jnp.stack([seq_index // NX, seq_index % NX, mp_index, core]).astype(jnp.int32)
    low_rim = jnp.stack([win_key[:WIN], win_value[:WIN]])
    high_rim = jnp.stack([win_key[WIN:], win_value[WIN:]])
    before = shifted(low_rim, "seq", 1)
    after = shifted(high_rim, "seq", -1)
    near, far, b7, b8 = gather_weight(w_query, core == 0)
    cross_dq, buffer = cross_call(
        cross_query, cross_dout, patch_key, patch_value, patch_len, patch_owner, seq_count
    )
    rows = gather_rows(cross_dq)
    win_dq, dk, dv, low_send, high_send = window_call(
        flags, win_query, win_dout, win_key, win_value, before, after
    )
    low_back = shifted(low_send, "seq", -1)
    high_back = shifted(high_send, "seq", 1)
    win_dk, win_dv = join_call(dk, dv, low_back, high_back)
    arrived = lax.all_to_all(buffer, "seq", split_axis=0, concat_axis=0, tiled=True)
    patch_grads = arrived.transpose(1, 0, 2, 3).reshape(2, -1, arrived.shape[3])
    byte_grads = product_call(pos, rows, near, far, b7, b8)
    return (win_dq, win_dk, win_dv, patch_grads, byte_grads)


def solution(mesh):
    tile = P("seq", "mp")
    rows = P("seq", None)
    in_specs = (tile,) * 8 + (rows, rows, tile)
    out_specs = (tile, tile, tile, P(None, "seq", "mp"), tile)
    return jax.shard_map(local, mesh=mesh, in_specs=in_specs, out_specs=out_specs, check_vma=False)
```

```python
import functools
import math

import jax
import jax.numpy as jnp
from jax import lax
from jax.experimental import pallas as pl
from jax.experimental.pallas import tpu as pltpu
from jax.sharding import Mesh
from jax.sharding import PartitionSpec as P

HD = 128
WIN = 256
INV_ROOT = 1.0 / math.sqrt(HD)
F32 = jnp.float32
BF16 = jnp.bfloat16


def dot(a, b, ca, cb):
    return lax.dot_general(a, b, (((ca,), (cb,)), ((), ())), preferred_element_type=F32)


def in_hbm(*arrays):
    return [pltpu.with_memory_space_constraint(a, pltpu.HBM) for a in arrays]


def window_block(q, do, k_rim, v_rim, k_own, v_own, rim_ok, own_ok):
    s_rim = jnp.where(rim_ok, dot(k_rim, q, 1, 1), -1e30)
    s_own = jnp.where(own_ok, dot(k_own, q, 1, 1), -1e30)
    top = jnp.maximum(
        jnp.max(s_rim, axis=0, keepdims=True), jnp.max(s_own, axis=0, keepdims=True)
    )
    e_rim = jnp.exp((s_rim - top) * INV_ROOT)
    e_own = jnp.exp((s_own - top) * INV_ROOT)
    scale = 1.0 / (
        jnp.sum(e_rim, axis=0, keepdims=True) + jnp.sum(e_own, axis=0, keepdims=True)
    )
    d_rim = dot(v_rim, do, 1, 1)
    d_own = dot(v_own, do, 1, 1)
    p_rim = e_rim * scale
    p_own = e_own * scale
    delta = jnp.sum(p_rim * d_rim, axis=0, keepdims=True) + jnp.sum(
        p_own * d_own, axis=0, keepdims=True
    )
    g_rim = (p_rim * (d_rim - delta) * INV_ROOT).astype(BF16)
    g_own = (p_own * (d_own - delta) * INV_ROOT).astype(BF16)
    p_rim = p_rim.astype(BF16)
    p_own = p_own.astype(BF16)
    dq = dot(g_rim, k_rim, 0, 0) + dot(g_own, k_own, 0, 0)
    return (
        dq,
        dot(g_rim, q, 1, 0),
        dot(p_rim, do, 1, 0),
        dot(g_own, q, 1, 0),
        dot(p_own, do, 1, 0),
    )


def window_kernel(
    flags, q_ref, do_ref, k_ref, v_ref, before_ref, after_ref,
    dq_ref, dk_ref, dv_ref, low_ref, high_ref,
):
    low_valid = flags[0]
    is_last = flags[1]
    rows = lax.broadcasted_iota(jnp.int32, (WIN, WIN), 0)
    cols = lax.broadcasted_iota(jnp.int32, (WIN, WIN), 1)
    rim_ok = rows >= cols
    own_ok = rows <= cols
    lo = slice(0, WIN)
    hi = slice(WIN, 2 * WIN)
    k_low, v_low = k_ref[lo, :], v_ref[lo, :]
    dq, dk_r, dv_r, dk_low, dv_low = window_block(
        q_ref[lo, :], do_ref[lo, :], before_ref[0], before_ref[1], k_low, v_low,
        rim_ok & (low_valid > 0), own_ok,
    )
    dq_ref[lo, :] = dq.astype(BF16)
    low_ref[0] = dk_r.astype(BF16)
    low_ref[1] = dv_r.astype(BF16)
    last = is_last > 0
    k_prev = jnp.where(last, k_low, after_ref[0])
    v_prev = jnp.where(last, v_low, after_ref[1])
    dq, dk_r, dv_r, dk_own, dv_own = window_block(
        q_ref[hi, :], do_ref[hi, :], k_prev, v_prev, k_ref[hi, :], v_ref[hi, :],
        rim_ok, own_ok,
    )
    dq_ref[hi, :] = dq.astype(BF16)
    high_ref[0] = dk_r.astype(BF16)
    high_ref[1] = dv_r.astype(BF16)
    dk_ref[hi, :] = dk_own
    dv_ref[hi, :] = dv_own
    dk_ref[lo, :] = dk_low + jnp.where(last, dk_r, 0.0)
    dv_ref[lo, :] = dv_low + jnp.where(last, dv_r, 0.0)


def window_call(flags, q, do, k, v, before, after):
    rows, width = q.shape
    full = pl.BlockSpec((rows, HD), lambda h, f: (0, h))
    rim = pl.BlockSpec((2, WIN, HD), lambda h, f: (0, 0, h))
    return pl.pallas_call(
        window_kernel,
        grid_spec=pltpu.PrefetchScalarGridSpec(
            num_scalar_prefetch=1,
            grid=(width // HD,),
            in_specs=[full] * 4 + [rim] * 2,
            out_specs=[full, full, full, rim, rim],
        ),
        out_shape=(
            jax.ShapeDtypeStruct((rows, width), BF16),
            jax.ShapeDtypeStruct((rows, width), F32),
            jax.ShapeDtypeStruct((rows, width), F32),
            jax.ShapeDtypeStruct((2, WIN, width), BF16),
            jax.ShapeDtypeStruct((2, WIN, width), BF16),
        ),
        name="window_grads",
        cost_estimate=pl.CostEstimate(flops=8_000_000_000, transcendentals=0, bytes_accessed=25_000_000),
        compiler_params=pltpu.CompilerParams(vmem_limit_bytes=40 << 20),
    )(flags, *in_hbm(q, do, k, v, before, after))


def cross_kernel(q_ref, do_ref, k_ref, v_ref, len_ref, owner_ref, dq_ref, buf_ref, sel_ref):
    blocks = len_ref.shape[0]
    per_block = len_ref.shape[1]
    rows = q_ref.shape[0] // blocks
    patches = blocks * per_block
    slots = sel_ref.shape[0]
    cap = buf_ref.shape[2]

    @pl.when(pl.program_id(0) == 0)
    def _():
        owner_col = jnp.broadcast_to(owner_ref[...], (patches, patches))
        owner_row = owner_col.T
        earlier = lax.broadcasted_iota(
            jnp.int32, (patches, patches), 0
        ) < lax.broadcasted_iota(jnp.int32, (patches, patches), 1)
        same = jnp.where((owner_col == owner_row) & earlier, 1, 0)
        rank = jnp.sum(same, axis=0, keepdims=True)
        slot = owner_ref[...] * cap + rank
        at = lax.broadcasted_iota(jnp.int32, (slots, patches), 0)
        sel_ref[...] = jnp.where(at == slot, 1.0, 0.0).astype(BF16)

    before = lax.broadcasted_iota(
        jnp.int32, (per_block, per_block), 1
    ) < lax.broadcasted_iota(jnp.int32, (per_block, per_block), 0)
    starts = dot(
        jnp.where(before, 1.0, 0.0).astype(BF16), len_ref[...].astype(F32).astype(BF16), 1, 1
    ).astype(jnp.int32)
    within = lax.broadcasted_iota(jnp.int32, (per_block, rows), 1)
    dks, dvs = [], []
    for b in range(blocks):
        r = slice(b * rows, (b + 1) * rows)
        p = slice(b * per_block, (b + 1) * per_block)
        q, do, k, v = q_ref[r, :], do_ref[r, :], k_ref[p, :], v_ref[p, :]
        ok = starts[:, b : b + 1] <= within
        s = jnp.where(ok, dot(k, q, 1, 1), -1e30)
        e = jnp.exp((s - jnp.max(s, axis=0, keepdims=True)) * INV_ROOT)
        probs = e * (1.0 / jnp.sum(e, axis=0, keepdims=True))
        d = dot(v, do, 1, 1)
        delta = jnp.sum(probs * d, axis=0, keepdims=True)
        g = (probs * (d - delta) * INV_ROOT).astype(BF16)
        dq = dot(g, k, 0, 0).astype(BF16)
        for i in range(dq_ref.shape[0]):
            dq_ref[i, r, :] = dq
        dks.append(dot(g, q, 1, 0).astype(BF16))
        dvs.append(dot(probs.astype(BF16), do, 1, 0).astype(BF16))
    sel = sel_ref[...]
    for i, parts in enumerate((dks, dvs)):
        placed = dot(sel, jnp.concatenate(parts, axis=0), 1, 0).astype(BF16)
        buf_ref[:, i] = placed.reshape(slots // cap, cap, HD)


def cross_call(q, do, k, v, lens, owners, owner_count, copies):
    rows, width = q.shape
    patches = k.shape[0]
    cap = max(2, 2 * (patches // owner_count))
    col = pl.BlockSpec((rows, HD), lambda h: (0, h))
    pcol = pl.BlockSpec((patches, HD), lambda h: (0, h))
    return pl.pallas_call(
        cross_kernel,
        grid_spec=pltpu.PrefetchScalarGridSpec(
            num_scalar_prefetch=0,
            grid=(width // HD,),
            in_specs=[
                col, col, pcol, pcol,
                pl.BlockSpec(lens.shape, lambda h: (0, 0)),
                pl.BlockSpec((1, patches), lambda h: (0, 0)),
            ],
            out_specs=[
                pl.BlockSpec((copies, rows, HD), lambda h: (0, 0, h)),
                pl.BlockSpec((owner_count, 2, cap, HD), lambda h: (0, 0, 0, h)),
            ],
            scratch_shapes=[pltpu.VMEM((owner_count * cap, patches), BF16)],
        ),
        out_shape=(
            jax.ShapeDtypeStruct((copies, rows, width), BF16),
            jax.ShapeDtypeStruct((owner_count, 2, cap, width), BF16),
        ),
        name="cross_grads",
        cost_estimate=pl.CostEstimate(flops=5_000_000_000, transcendentals=0, bytes_accessed=15_000_000),
        compiler_params=pltpu.CompilerParams(vmem_limit_bytes=40 << 20),
    )(*in_hbm(q, do, k, v, lens, owners.reshape(1, patches)))


def join_kernel(dk_ref, dv_ref, low_ref, high_ref, dk_out, dv_out):
    for i, (src, out) in enumerate(((dk_ref, dk_out), (dv_ref, dv_out))):
        out[:WIN, :] = (src[:WIN, :] + low_ref[i].astype(F32)).astype(BF16)
        out[WIN:, :] = (src[WIN:, :] + high_ref[i].astype(F32)).astype(BF16)


def join_call(dk, dv, low_back, high_back):
    rows, width = dk.shape
    step = 2 * HD
    col = pl.BlockSpec((rows, step), lambda h: (0, h))
    rim = pl.BlockSpec((2, WIN, step), lambda h: (0, 0, h))
    out = jax.ShapeDtypeStruct((rows, width), BF16)
    return pl.pallas_call(
        join_kernel,
        grid=(width // step,),
        in_specs=[col, col, rim, rim],
        out_specs=[col, col],
        out_shape=(out, out),
        name="join_rims",
        compiler_params=pltpu.CompilerParams(vmem_limit_bytes=40 << 20),
    )(*in_hbm(dk, dv, low_back, high_back))


def pack_kernel(k_ref, v_ref, low_ref, high_ref):
    for i, ref in enumerate((k_ref, v_ref)):
        low_ref[i] = ref[:WIN, :]
        high_ref[i] = ref[WIN:, :]


def pack_call(k, v):
    rows, width = k.shape
    step = 2 * HD
    full = pl.BlockSpec((rows, step), lambda h: (0, h))
    rim = pl.BlockSpec((2, WIN, step), lambda h: (0, 0, h))
    out = jax.ShapeDtypeStruct((2, WIN, width), BF16)
    return pl.pallas_call(
        pack_kernel,
        grid=(width // step,),
        in_specs=[full] * 2,
        out_specs=[rim, rim],
        out_shape=(out, out),
        name="pack_rims",
    )(*in_hbm(k, v))


def shifted(block, axis, distance):
    devices = range(lax.axis_size(axis))
    route = [(i - distance, i) for i in devices if i - distance in devices]
    return lax.ppermute(block, axis, route)


NZ, NX, NY, NC = 8, 4, 4, 2
AXES = ("z", "x", "y", "core")
SEQ = ("z", "x")


def place(z, x, y, c):
    return ((z % NZ) * NX + x % NX) * (NY * NC) + (y % NY) * NC + c


def send(block, target):
    route = []
    for z in range(NZ):
        for x in range(NX):
            for y in range(NY):
                for c in range(NC):
                    route.append((place(z, x, y, c), place(*target(z, x, y, c))))
    return lax.ppermute(block, AXES, route)


def product_kernel(pos, own_ref, other_ref, w_own_ref, w_other_ref, out_ref, total_ref):
    step = pl.program_id(0)
    part = dot(own_ref[0], w_own_ref[0], 1, 1) + dot(other_ref[0], w_other_ref[0], 1, 1)

    @pl.when(step == 0)
    def _():
        total_ref[...] = part

    @pl.when(step > 0)
    def _():
        total_ref[...] += part

    @pl.when(step == pl.num_programs(0) - 1)
    def _():
        out_ref[...] = total_ref[...].astype(BF16)


def product_call(pos, own_rows, other_rows, whole):
    count, width = own_rows.shape[1:]
    n_rows = whole.shape[1]
    rows = pl.BlockSpec((1, count, width), lambda i, p: (i, 0, 0))
    return pl.pallas_call(
        product_kernel,
        grid_spec=pltpu.PrefetchScalarGridSpec(
            num_scalar_prefetch=1,
            grid=(NY,),
            in_specs=[
                rows, rows,
                pl.BlockSpec(
                    (1, n_rows, width), lambda i, p: (lax.rem(NC * i + p[2] + p[1], NZ), 0, 0)
                ),
                pl.BlockSpec(
                    (1, n_rows, width), lambda i, p: (lax.rem(NC * i + 1 - p[2] + p[1], NZ), 0, 0)
                ),
            ],
            out_specs=pl.BlockSpec((count, n_rows), lambda i, p: (0, 0)),
            scratch_shapes=[pltpu.VMEM((count, n_rows), F32)],
        ),
        out_shape=jax.ShapeDtypeStruct((count, n_rows), BF16),
        name="byte_product",
        compiler_params=pltpu.CompilerParams(vmem_limit_bytes=40 << 20),
    )(pos, *in_hbm(own_rows, other_rows, whole, whole))


def local(
    win_query, win_key, win_value, win_dout, cross_query, cross_dout,
    patch_key, patch_value, patch_len, patch_owner, w_query,
):
    z, x = lax.axis_index("z"), lax.axis_index("x")
    y, core = lax.axis_index("y"), lax.axis_index("core")
    seq_count = NZ * NX
    seq_index = z * NX + x
    flags = jnp.stack([seq_index > 0, seq_index == seq_count - 1]).astype(jnp.int32)
    pos = jnp.stack([x, y * NC + core, core]).astype(jnp.int32)
    own = send(w_query, lambda z, x, y, c: (z + NC * y + c, x, z // NC, z % NC))
    low_rim, high_rim = pack_call(win_key, win_value)
    cross_query, low_rim = lax.optimization_barrier((cross_query, low_rim))
    cross_dq, buffer = cross_call(
        cross_query, cross_dout, patch_key, patch_value, patch_len, patch_owner, seq_count, NY
    )
    own, cross_dq, buffer, low_rim, high_rim = lax.optimization_barrier(
        (own, cross_dq, buffer, low_rim, high_rim)
    )
    whole = lax.all_gather(own, SEQ, axis=0, tiled=True)
    whole = whole.reshape(NZ, NX * own.shape[0], own.shape[1])
    before = shifted(low_rim, SEQ, 1)
    after = shifted(high_rim, SEQ, -1)
    own_rows = lax.all_to_all(cross_dq, "y", split_axis=0, concat_axis=0, tiled=True)
    win_dq, dk, dv, low_send, high_send = window_call(
        flags, win_query, win_dout, win_key, win_value, before, after
    )
    win_dq, buffer = lax.optimization_barrier((win_dq, buffer))
    arrived = lax.all_to_all(buffer, SEQ, split_axis=0, concat_axis=0, tiled=True)
    low_back = shifted(low_send, SEQ, -1)
    high_back = shifted(high_send, SEQ, 1)
    low_back, high_back, own_rows = lax.optimization_barrier((low_back, high_back, own_rows))
    other_rows = send(own_rows, lambda z, x, y, c: (z, x, y, 1 - c))
    win_dk, win_dv = join_call(dk, dv, low_back, high_back)
    arrived, win_dk = lax.optimization_barrier((arrived, win_dk))
    patch_grads = arrived.transpose(1, 0, 2, 3).reshape(2, -1, arrived.shape[3])
    byte_grads = product_call(pos, own_rows, other_rows, whole)
    return (win_dq, win_dk, win_dv, patch_grads, byte_grads)


def solution(mesh):
    mesh = Mesh(mesh.devices.reshape(NZ, NX, NY, NC), AXES)
    mp = ("y", "core")
    tile = P(SEQ, mp)
    rows = P(SEQ, None)
    in_specs = (tile,) * 8 + (rows, rows, tile)
    out_specs = (tile, tile, tile, P(None, SEQ, mp), tile)
    return jax.shard_map(local, mesh=mesh, in_specs=in_specs, out_specs=out_specs, check_vma=False)
```

```python
import functools
import math

import jax
import jax.numpy as jnp
from jax import lax
from jax.experimental import pallas as pl
from jax.experimental.pallas import tpu as pltpu
from jax.sharding import Mesh
from jax.sharding import PartitionSpec as P

HD = 128
WIN = 256
INV_ROOT = 1.0 / math.sqrt(HD)
F32 = jnp.float32
BF16 = jnp.bfloat16


def dot(a, b, ca, cb):
    return lax.dot_general(a, b, (((ca,), (cb,)), ((), ())), preferred_element_type=F32)


def in_hbm(*arrays):
    return [pltpu.with_memory_space_constraint(a, pltpu.HBM) for a in arrays]


def window_block(q, do, k_rim, v_rim, k_own, v_own, rim_ok, own_ok):
    s_rim = jnp.where(rim_ok, dot(k_rim, q, 1, 1), -1e30)
    s_own = jnp.where(own_ok, dot(k_own, q, 1, 1), -1e30)
    top = jnp.maximum(
        jnp.max(s_rim, axis=0, keepdims=True), jnp.max(s_own, axis=0, keepdims=True)
    )
    e_rim = jnp.exp((s_rim - top) * INV_ROOT)
    e_own = jnp.exp((s_own - top) * INV_ROOT)
    scale = 1.0 / (
        jnp.sum(e_rim, axis=0, keepdims=True) + jnp.sum(e_own, axis=0, keepdims=True)
    )
    d_rim = dot(v_rim, do, 1, 1)
    d_own = dot(v_own, do, 1, 1)
    p_rim = e_rim * scale
    p_own = e_own * scale
    delta = jnp.sum(p_rim * d_rim, axis=0, keepdims=True) + jnp.sum(
        p_own * d_own, axis=0, keepdims=True
    )
    g_rim = (p_rim * (d_rim - delta) * INV_ROOT).astype(BF16)
    g_own = (p_own * (d_own - delta) * INV_ROOT).astype(BF16)
    p_rim = p_rim.astype(BF16)
    p_own = p_own.astype(BF16)
    dq = dot(g_rim, k_rim, 0, 0) + dot(g_own, k_own, 0, 0)
    return (
        dq,
        dot(g_rim, q, 1, 0),
        dot(p_rim, do, 1, 0),
        dot(g_own, q, 1, 0),
        dot(p_own, do, 1, 0),
    )


def window_kernel(
    flags, q_ref, do_ref, k_ref, v_ref, before_ref, after_ref,
    dq_ref, dk_ref, dv_ref, low_ref, high_ref,
):
    low_valid = flags[0]
    is_last = flags[1]
    rows = lax.broadcasted_iota(jnp.int32, (WIN, WIN), 0)
    cols = lax.broadcasted_iota(jnp.int32, (WIN, WIN), 1)
    rim_ok = rows >= cols
    own_ok = rows <= cols
    lo = slice(0, WIN)
    hi = slice(WIN, 2 * WIN)
    k_low, v_low = k_ref[lo, :], v_ref[lo, :]
    dq, dk_r, dv_r, dk_low, dv_low = window_block(
        q_ref[lo, :], do_ref[lo, :], before_ref[0], before_ref[1], k_low, v_low,
        rim_ok & (low_valid > 0), own_ok,
    )
    dq_ref[lo, :] = dq.astype(BF16)
    low_ref[0] = dk_r.astype(BF16)
    low_ref[1] = dv_r.astype(BF16)
    last = is_last > 0
    k_prev = jnp.where(last, k_low, after_ref[0])
    v_prev = jnp.where(last, v_low, after_ref[1])
    dq, dk_r, dv_r, dk_own, dv_own = window_block(
        q_ref[hi, :], do_ref[hi, :], k_prev, v_prev, k_ref[hi, :], v_ref[hi, :],
        rim_ok, own_ok,
    )
    dq_ref[hi, :] = dq.astype(BF16)
    high_ref[0] = dk_r.astype(BF16)
    high_ref[1] = dv_r.astype(BF16)
    dk_ref[hi, :] = dk_own
    dv_ref[hi, :] = dv_own
    dk_ref[lo, :] = dk_low + jnp.where(last, dk_r, 0.0)
    dv_ref[lo, :] = dv_low + jnp.where(last, dv_r, 0.0)


def window_call(flags, q, do, k, v, before, after):
    rows, width = q.shape
    full = pl.BlockSpec((rows, HD), lambda h, f: (0, h))
    rim = pl.BlockSpec((2, WIN, HD), lambda h, f: (0, 0, h))
    return pl.pallas_call(
        window_kernel,
        grid_spec=pltpu.PrefetchScalarGridSpec(
            num_scalar_prefetch=1,
            grid=(width // HD,),
            in_specs=[full] * 4 + [rim] * 2,
            out_specs=[full, full, full, rim, rim],
        ),
        out_shape=(
            jax.ShapeDtypeStruct((rows, width), BF16),
            jax.ShapeDtypeStruct((rows, width), F32),
            jax.ShapeDtypeStruct((rows, width), F32),
            jax.ShapeDtypeStruct((2, WIN, width), BF16),
            jax.ShapeDtypeStruct((2, WIN, width), BF16),
        ),
        name="window_grads",
        cost_estimate=pl.CostEstimate(flops=8_000_000_000, transcendentals=0, bytes_accessed=25_000_000),
        compiler_params=pltpu.CompilerParams(vmem_limit_bytes=40 << 20),
    )(flags, *in_hbm(q, do, k, v, before, after))


def cross_kernel(q_ref, do_ref, k_ref, v_ref, len_ref, owner_ref, dq_ref, buf_ref, sel_ref):
    blocks = len_ref.shape[0]
    per_block = len_ref.shape[1]
    rows = q_ref.shape[0] // blocks
    patches = blocks * per_block
    slots = sel_ref.shape[0]
    cap = buf_ref.shape[2]

    @pl.when(pl.program_id(0) == 0)
    def _():
        owner_col = jnp.broadcast_to(owner_ref[...], (patches, patches))
        owner_row = owner_col.T
        earlier = lax.broadcasted_iota(
            jnp.int32, (patches, patches), 0
        ) < lax.broadcasted_iota(jnp.int32, (patches, patches), 1)
        same = jnp.where((owner_col == owner_row) & earlier, 1, 0)
        rank = jnp.sum(same, axis=0, keepdims=True)
        slot = owner_ref[...] * cap + rank
        at = lax.broadcasted_iota(jnp.int32, (slots, patches), 0)
        sel_ref[...] = jnp.where(at == slot, 1.0, 0.0).astype(BF16)

    before = lax.broadcasted_iota(
        jnp.int32, (per_block, per_block), 1
    ) < lax.broadcasted_iota(jnp.int32, (per_block, per_block), 0)
    starts = dot(
        jnp.where(before, 1.0, 0.0).astype(BF16), len_ref[...].astype(F32).astype(BF16), 1, 1
    ).astype(jnp.int32)
    within = lax.broadcasted_iota(jnp.int32, (per_block, rows), 1)
    dks, dvs = [], []
    for b in range(blocks):
        r = slice(b * rows, (b + 1) * rows)
        p = slice(b * per_block, (b + 1) * per_block)
        q, do, k, v = q_ref[r, :], do_ref[r, :], k_ref[p, :], v_ref[p, :]
        ok = starts[:, b : b + 1] <= within
        s = jnp.where(ok, dot(k, q, 1, 1), -1e30)
        e = jnp.exp((s - jnp.max(s, axis=0, keepdims=True)) * INV_ROOT)
        probs = e * (1.0 / jnp.sum(e, axis=0, keepdims=True))
        d = dot(v, do, 1, 1)
        delta = jnp.sum(probs * d, axis=0, keepdims=True)
        g = (probs * (d - delta) * INV_ROOT).astype(BF16)
        dq = dot(g, k, 0, 0).astype(BF16)
        for i in range(dq_ref.shape[0]):
            dq_ref[i, r, :] = dq
        dks.append(dot(g, q, 1, 0).astype(BF16))
        dvs.append(dot(probs.astype(BF16), do, 1, 0).astype(BF16))
    sel = sel_ref[...]
    for i, parts in enumerate((dks, dvs)):
        placed = dot(sel, jnp.concatenate(parts, axis=0), 1, 0).astype(BF16)
        buf_ref[:, i] = placed.reshape(slots // cap, cap, HD)


def cross_call(q, do, k, v, lens, owners, owner_count, copies):
    rows, width = q.shape
    patches = k.shape[0]
    cap = max(2, 2 * (patches // owner_count))
    col = pl.BlockSpec((rows, HD), lambda h: (0, h))
    pcol = pl.BlockSpec((patches, HD), lambda h: (0, h))
    return pl.pallas_call(
        cross_kernel,
        grid_spec=pltpu.PrefetchScalarGridSpec(
            num_scalar_prefetch=0,
            grid=(width // HD,),
            in_specs=[
                col, col, pcol, pcol,
                pl.BlockSpec(lens.shape, lambda h: (0, 0)),
                pl.BlockSpec((1, patches), lambda h: (0, 0)),
            ],
            out_specs=[
                pl.BlockSpec((copies, rows, HD), lambda h: (0, 0, h)),
                pl.BlockSpec((owner_count, 2, cap, HD), lambda h: (0, 0, 0, h)),
            ],
            scratch_shapes=[pltpu.VMEM((owner_count * cap, patches), BF16)],
        ),
        out_shape=(
            jax.ShapeDtypeStruct((copies, rows, width), BF16),
            jax.ShapeDtypeStruct((owner_count, 2, cap, width), BF16),
        ),
        name="cross_grads",
        cost_estimate=pl.CostEstimate(flops=5_000_000_000, transcendentals=0, bytes_accessed=15_000_000),
        compiler_params=pltpu.CompilerParams(vmem_limit_bytes=40 << 20),
    )(*in_hbm(q, do, k, v, lens, owners.reshape(1, patches)))


def join_kernel(dk_ref, dv_ref, low_ref, high_ref, dk_out, dv_out):
    for i, (src, out) in enumerate(((dk_ref, dk_out), (dv_ref, dv_out))):
        out[:WIN, :] = (src[:WIN, :] + low_ref[i].astype(F32)).astype(BF16)
        out[WIN:, :] = (src[WIN:, :] + high_ref[i].astype(F32)).astype(BF16)


def join_call(dk, dv, low_back, high_back):
    rows, width = dk.shape
    step = 2 * HD
    col = pl.BlockSpec((rows, step), lambda h: (0, h))
    rim = pl.BlockSpec((2, WIN, step), lambda h: (0, 0, h))
    out = jax.ShapeDtypeStruct((rows, width), BF16)
    return pl.pallas_call(
        join_kernel,
        grid=(width // step,),
        in_specs=[col, col, rim, rim],
        out_specs=[col, col],
        out_shape=(out, out),
        name="join_rims",
        compiler_params=pltpu.CompilerParams(vmem_limit_bytes=40 << 20),
    )(*in_hbm(dk, dv, low_back, high_back))


def pack_kernel(k_ref, v_ref, low_ref, high_ref):
    for i, ref in enumerate((k_ref, v_ref)):
        low_ref[i] = ref[:WIN, :]
        high_ref[i] = ref[WIN:, :]


def pack_call(k, v):
    rows, width = k.shape
    step = 2 * HD
    full = pl.BlockSpec((rows, step), lambda h: (0, h))
    rim = pl.BlockSpec((2, WIN, step), lambda h: (0, 0, h))
    out = jax.ShapeDtypeStruct((2, WIN, width), BF16)
    return pl.pallas_call(
        pack_kernel,
        grid=(width // step,),
        in_specs=[full] * 2,
        out_specs=[rim, rim],
        out_shape=(out, out),
        name="pack_rims",
    )(*in_hbm(k, v))


def shifted(block, axis, distance):
    devices = range(lax.axis_size(axis))
    route = [(i - distance, i) for i in devices if i - distance in devices]
    return lax.ppermute(block, axis, route)


NZ, NX, NY, NC = 8, 4, 4, 2
AXES = ("z", "x", "y", "core")
SEQ = ("z", "x")


def place(z, x, y, c):
    return ((z % NZ) * NX + x % NX) * (NY * NC) + (y % NY) * NC + c


def send(block, target):
    route = []
    for z in range(NZ):
        for x in range(NX):
            for y in range(NY):
                for c in range(NC):
                    route.append((place(z, x, y, c), place(*target(z, x, y, c))))
    return lax.ppermute(block, AXES, route)


def product_kernel(
    pos, own_ref, other_ref, whole_ref, out_ref, a_buf, w_buf, a_sem, w_sem
):
    m, c = pos[1], pos[2]
    copies = []
    for j in range(NZ):
        rows, core = (own_ref, c) if j % NC == 0 else (other_ref, 1 - c)
        slot = lax.rem(NC * (j // NC) + core + m, NZ)
        copies.append(
            (
                pltpu.make_async_copy(rows.at[j // NC], a_buf.at[j], a_sem.at[j]),
                pltpu.make_async_copy(whole_ref.at[slot], w_buf.at[j], w_sem.at[j]),
            )
        )
    for rows, weight in copies:
        rows.start()
        weight.start()
    total = None
    for j, (rows, weight) in enumerate(copies):
        rows.wait()
        weight.wait()
        part = dot(a_buf[j], w_buf[j], 1, 1)
        total = part if total is None else total + part
    out_ref[...] = total.astype(BF16)


def product_call(pos, own_rows, other_rows, whole):
    count, width = own_rows.shape[1:]
    n_rows = whole.shape[1]
    anywhere = pl.BlockSpec(memory_space=pl.ANY)
    return pl.pallas_call(
        product_kernel,
        grid_spec=pltpu.PrefetchScalarGridSpec(
            num_scalar_prefetch=1,
            grid=(1,),
            in_specs=[anywhere] * 3,
            out_specs=pl.BlockSpec((count, n_rows), lambda i, p: (0, 0)),
            scratch_shapes=[
                pltpu.VMEM((NZ, count, width), BF16),
                pltpu.VMEM((NZ, n_rows, width), BF16),
                pltpu.SemaphoreType.DMA((NZ,)),
                pltpu.SemaphoreType.DMA((NZ,)),
            ],
        ),
        out_shape=jax.ShapeDtypeStruct((count, n_rows), BF16),
        name="byte_product",
        compiler_params=pltpu.CompilerParams(vmem_limit_bytes=40 << 20),
    )(pos, *in_hbm(own_rows, other_rows, whole))


def local(
    win_query, win_key, win_value, win_dout, cross_query, cross_dout,
    patch_key, patch_value, patch_len, patch_owner, w_query,
):
    z, x = lax.axis_index("z"), lax.axis_index("x")
    y, core = lax.axis_index("y"), lax.axis_index("core")
    seq_count = NZ * NX
    seq_index = z * NX + x
    flags = jnp.stack([seq_index > 0, seq_index == seq_count - 1]).astype(jnp.int32)
    pos = jnp.stack([x, y * NC + core, core]).astype(jnp.int32)
    own = send(w_query, lambda z, x, y, c: (z + NC * y + c, x, z // NC, z % NC))
    low_rim, high_rim = pack_call(win_key, win_value)
    cross_query, low_rim = lax.optimization_barrier((cross_query, low_rim))
    cross_dq, buffer = cross_call(
        cross_query, cross_dout, patch_key, patch_value, patch_len, patch_owner, seq_count, NY
    )
    own, cross_dq, buffer, low_rim, high_rim = lax.optimization_barrier(
        (own, cross_dq, buffer, low_rim, high_rim)
    )
    whole = lax.all_gather(own, SEQ, axis=0, tiled=True)
    whole = whole.reshape(NZ, NX * own.shape[0], own.shape[1])
    before = shifted(low_rim, SEQ, 1)
    after = shifted(high_rim, SEQ, -1)
    own_rows = lax.all_to_all(cross_dq, "y", split_axis=0, concat_axis=0, tiled=True)
    win_dq, dk, dv, low_send, high_send = window_call(
        flags, win_query, win_dout, win_key, win_value, before, after
    )
    win_dq, buffer = lax.optimization_barrier((win_dq, buffer))
    arrived = lax.all_to_all(buffer, SEQ, split_axis=0, concat_axis=0, tiled=True)
    low_back = shifted(low_send, SEQ, -1)
    high_back = shifted(high_send, SEQ, 1)
    low_back, high_back, own_rows = lax.optimization_barrier((low_back, high_back, own_rows))
    other_rows = send(own_rows, lambda z, x, y, c: (z, x, y, 1 - c))
    win_dk, win_dv = join_call(dk, dv, low_back, high_back)
    arrived, win_dk = lax.optimization_barrier((arrived, win_dk))
    patch_grads = arrived.transpose(1, 0, 2, 3).reshape(2, -1, arrived.shape[3])
    byte_grads = product_call(pos, own_rows, other_rows, whole)
    return (win_dq, win_dk, win_dv, patch_grads, byte_grads)


def solution(mesh):
    mesh = Mesh(mesh.devices.reshape(NZ, NX, NY, NC), AXES)
    mp = ("y", "core")
    tile = P(SEQ, mp)
    rows = P(SEQ, None)
    in_specs = (tile,) * 8 + (rows, rows, tile)
    out_specs = (tile, tile, tile, P(None, SEQ, mp), tile)
    return jax.shard_map(local, mesh=mesh, in_specs=in_specs, out_specs=out_specs, check_vma=False)
```

```python
import functools
import math

import jax
import jax.numpy as jnp
from jax import lax
from jax.experimental import pallas as pl
from jax.experimental.pallas import tpu as pltpu
from jax.sharding import Mesh
from jax.sharding import PartitionSpec as P

HD = 128
WIN = 256
INV_ROOT = 1.0 / math.sqrt(HD)
F32 = jnp.float32
BF16 = jnp.bfloat16


def dot(a, b, ca, cb):
    return lax.dot_general(a, b, (((ca,), (cb,)), ((), ())), preferred_element_type=F32)


def in_hbm(*arrays):
    return [pltpu.with_memory_space_constraint(a, pltpu.HBM) for a in arrays]


def window_block(q, do, k_rim, v_rim, k_own, v_own, rim_ok, own_ok):
    s_rim = jnp.where(rim_ok, dot(k_rim, q, 1, 1), -1e30)
    s_own = jnp.where(own_ok, dot(k_own, q, 1, 1), -1e30)
    top = jnp.maximum(
        jnp.max(s_rim, axis=0, keepdims=True), jnp.max(s_own, axis=0, keepdims=True)
    )
    e_rim = jnp.exp((s_rim - top) * INV_ROOT)
    e_own = jnp.exp((s_own - top) * INV_ROOT)
    scale = 1.0 / (
        jnp.sum(e_rim, axis=0, keepdims=True) + jnp.sum(e_own, axis=0, keepdims=True)
    )
    d_rim = dot(v_rim, do, 1, 1)
    d_own = dot(v_own, do, 1, 1)
    p_rim = e_rim * scale
    p_own = e_own * scale
    delta = jnp.sum(p_rim * d_rim, axis=0, keepdims=True) + jnp.sum(
        p_own * d_own, axis=0, keepdims=True
    )
    g_rim = (p_rim * (d_rim - delta) * INV_ROOT).astype(BF16)
    g_own = (p_own * (d_own - delta) * INV_ROOT).astype(BF16)
    p_rim = p_rim.astype(BF16)
    p_own = p_own.astype(BF16)
    dq = dot(g_rim, k_rim, 0, 0) + dot(g_own, k_own, 0, 0)
    return (
        dq,
        dot(g_rim, q, 1, 0),
        dot(p_rim, do, 1, 0),
        dot(g_own, q, 1, 0),
        dot(p_own, do, 1, 0),
    )


def window_kernel(
    flags, q_ref, do_ref, k_ref, v_ref, before_ref, after_ref,
    dq_ref, dk_ref, dv_ref, low_ref, high_ref,
):
    low_valid = flags[0]
    is_last = flags[1]
    rows = lax.broadcasted_iota(jnp.int32, (WIN, WIN), 0)
    cols = lax.broadcasted_iota(jnp.int32, (WIN, WIN), 1)
    rim_ok = rows >= cols
    own_ok = rows <= cols
    lo = slice(0, WIN)
    hi = slice(WIN, 2 * WIN)
    k_low, v_low = k_ref[lo, :], v_ref[lo, :]
    dq, dk_r, dv_r, dk_low, dv_low = window_block(
        q_ref[lo, :], do_ref[lo, :], before_ref[0], before_ref[1], k_low, v_low,
        rim_ok & (low_valid > 0), own_ok,
    )
    dq_ref[lo, :] = dq.astype(BF16)
    low_ref[0] = dk_r.astype(BF16)
    low_ref[1] = dv_r.astype(BF16)
    last = is_last > 0
    k_prev = jnp.where(last, k_low, after_ref[0])
    v_prev = jnp.where(last, v_low, after_ref[1])
    dq, dk_r, dv_r, dk_own, dv_own = window_block(
        q_ref[hi, :], do_ref[hi, :], k_prev, v_prev, k_ref[hi, :], v_ref[hi, :],
        rim_ok, own_ok,
    )
    dq_ref[hi, :] = dq.astype(BF16)
    high_ref[0] = dk_r.astype(BF16)
    high_ref[1] = dv_r.astype(BF16)
    dk_ref[hi, :] = dk_own
    dv_ref[hi, :] = dv_own
    dk_ref[lo, :] = dk_low + jnp.where(last, dk_r, 0.0)
    dv_ref[lo, :] = dv_low + jnp.where(last, dv_r, 0.0)


def window_call(flags, q, do, k, v, before, after):
    rows, width = q.shape
    full = pl.BlockSpec((rows, HD), lambda h, f: (0, h))
    rim = pl.BlockSpec((2, WIN, HD), lambda h, f: (0, 0, h))
    return pl.pallas_call(
        window_kernel,
        grid_spec=pltpu.PrefetchScalarGridSpec(
            num_scalar_prefetch=1,
            grid=(width // HD,),
            in_specs=[full] * 4 + [rim] * 2,
            out_specs=[full, full, full, rim, rim],
        ),
        out_shape=(
            jax.ShapeDtypeStruct((rows, width), BF16),
            jax.ShapeDtypeStruct((rows, width), F32),
            jax.ShapeDtypeStruct((rows, width), F32),
            jax.ShapeDtypeStruct((2, WIN, width), BF16),
            jax.ShapeDtypeStruct((2, WIN, width), BF16),
        ),
        name="window_grads",
        cost_estimate=pl.CostEstimate(flops=8_000_000_000, transcendentals=0, bytes_accessed=25_000_000),
        compiler_params=pltpu.CompilerParams(vmem_limit_bytes=40 << 20),
    )(flags, *in_hbm(q, do, k, v, before, after))


def cross_kernel(q_ref, do_ref, k_ref, v_ref, len_ref, owner_ref, dq_ref, buf_ref, sel_ref):
    blocks = len_ref.shape[0]
    per_block = len_ref.shape[1]
    rows = q_ref.shape[0] // blocks
    patches = blocks * per_block
    slots = sel_ref.shape[0]
    cap = buf_ref.shape[2]

    @pl.when(pl.program_id(0) == 0)
    def _():
        owner_col = jnp.broadcast_to(owner_ref[...], (patches, patches))
        owner_row = owner_col.T
        earlier = lax.broadcasted_iota(
            jnp.int32, (patches, patches), 0
        ) < lax.broadcasted_iota(jnp.int32, (patches, patches), 1)
        same = jnp.where((owner_col == owner_row) & earlier, 1, 0)
        rank = jnp.sum(same, axis=0, keepdims=True)
        slot = owner_ref[...] * cap + rank
        at = lax.broadcasted_iota(jnp.int32, (slots, patches), 0)
        sel_ref[...] = jnp.where(at == slot, 1.0, 0.0).astype(BF16)

    before = lax.broadcasted_iota(
        jnp.int32, (per_block, per_block), 1
    ) < lax.broadcasted_iota(jnp.int32, (per_block, per_block), 0)
    starts = dot(
        jnp.where(before, 1.0, 0.0).astype(BF16), len_ref[...].astype(F32).astype(BF16), 1, 1
    ).astype(jnp.int32)
    within = lax.broadcasted_iota(jnp.int32, (per_block, rows), 1)
    dks, dvs = [], []
    for b in range(blocks):
        r = slice(b * rows, (b + 1) * rows)
        p = slice(b * per_block, (b + 1) * per_block)
        q, do, k, v = q_ref[r, :], do_ref[r, :], k_ref[p, :], v_ref[p, :]
        ok = starts[:, b : b + 1] <= within
        s = jnp.where(ok, dot(k, q, 1, 1), -1e30)
        e = jnp.exp((s - jnp.max(s, axis=0, keepdims=True)) * INV_ROOT)
        probs = e * (1.0 / jnp.sum(e, axis=0, keepdims=True))
        d = dot(v, do, 1, 1)
        delta = jnp.sum(probs * d, axis=0, keepdims=True)
        g = (probs * (d - delta) * INV_ROOT).astype(BF16)
        dq = dot(g, k, 0, 0).astype(BF16)
        for i in range(dq_ref.shape[0]):
            dq_ref[i, r, :] = dq
        dks.append(dot(g, q, 1, 0).astype(BF16))
        dvs.append(dot(probs.astype(BF16), do, 1, 0).astype(BF16))
    sel = sel_ref[...]
    for i, parts in enumerate((dks, dvs)):
        placed = dot(sel, jnp.concatenate(parts, axis=0), 1, 0).astype(BF16)
        buf_ref[:, i] = placed.reshape(slots // cap, cap, HD)


def cross_call(q, do, k, v, lens, owners, owner_count, copies):
    rows, width = q.shape
    patches = k.shape[0]
    cap = max(2, 2 * (patches // owner_count))
    col = pl.BlockSpec((rows, HD), lambda h: (0, h))
    pcol = pl.BlockSpec((patches, HD), lambda h: (0, h))
    return pl.pallas_call(
        cross_kernel,
        grid_spec=pltpu.PrefetchScalarGridSpec(
            num_scalar_prefetch=0,
            grid=(width // HD,),
            in_specs=[
                col, col, pcol, pcol,
                pl.BlockSpec(lens.shape, lambda h: (0, 0)),
                pl.BlockSpec((1, patches), lambda h: (0, 0)),
            ],
            out_specs=[
                pl.BlockSpec((copies, rows, HD), lambda h: (0, 0, h)),
                pl.BlockSpec((owner_count, 2, cap, HD), lambda h: (0, 0, 0, h)),
            ],
            scratch_shapes=[pltpu.VMEM((owner_count * cap, patches), BF16)],
        ),
        out_shape=(
            jax.ShapeDtypeStruct((copies, rows, width), BF16),
            jax.ShapeDtypeStruct((owner_count, 2, cap, width), BF16),
        ),
        name="cross_grads",
        cost_estimate=pl.CostEstimate(flops=5_000_000_000, transcendentals=0, bytes_accessed=15_000_000),
        compiler_params=pltpu.CompilerParams(vmem_limit_bytes=40 << 20),
    )(*in_hbm(q, do, k, v, lens, owners.reshape(1, patches)))


def join_kernel(dk_ref, dv_ref, low_ref, high_ref, dk_out, dv_out):
    for i, (src, out) in enumerate(((dk_ref, dk_out), (dv_ref, dv_out))):
        out[:WIN, :] = (src[:WIN, :] + low_ref[i].astype(F32)).astype(BF16)
        out[WIN:, :] = (src[WIN:, :] + high_ref[i].astype(F32)).astype(BF16)


def join_call(dk, dv, low_back, high_back):
    rows, width = dk.shape
    step = 2 * HD
    col = pl.BlockSpec((rows, step), lambda h: (0, h))
    rim = pl.BlockSpec((2, WIN, step), lambda h: (0, 0, h))
    out = jax.ShapeDtypeStruct((rows, width), BF16)
    return pl.pallas_call(
        join_kernel,
        grid=(width // step,),
        in_specs=[col, col, rim, rim],
        out_specs=[col, col],
        out_shape=(out, out),
        name="join_rims",
        compiler_params=pltpu.CompilerParams(vmem_limit_bytes=40 << 20),
    )(*in_hbm(dk, dv, low_back, high_back))


def pack_kernel(k_ref, v_ref, low_ref, high_ref):
    for i, ref in enumerate((k_ref, v_ref)):
        low_ref[i] = ref[:WIN, :]
        high_ref[i] = ref[WIN:, :]


def pack_call(k, v):
    rows, width = k.shape
    step = 2 * HD
    full = pl.BlockSpec((rows, step), lambda h: (0, h))
    rim = pl.BlockSpec((2, WIN, step), lambda h: (0, 0, h))
    out = jax.ShapeDtypeStruct((2, WIN, width), BF16)
    return pl.pallas_call(
        pack_kernel,
        grid=(width // step,),
        in_specs=[full] * 2,
        out_specs=[rim, rim],
        out_shape=(out, out),
        name="pack_rims",
    )(*in_hbm(k, v))


def shifted(block, axis, distance):
    devices = range(lax.axis_size(axis))
    route = [(i - distance, i) for i in devices if i - distance in devices]
    return lax.ppermute(block, axis, route)


NZ, NX, NY, NC = 8, 4, 4, 2
AXES = ("z", "x", "y", "core")
SEQ = ("z", "x")
SHIFTS = (0, 1, -1, 2)


def place(z, x, y, c):
    return ((z % NZ) * NX + x % NX) * (NY * NC) + (y % NY) * NC + c


def send(block, target):
    route = []
    for z in range(NZ):
        for x in range(NX):
            for y in range(NY):
                for c in range(NC):
                    route.append((place(z, x, y, c), place(*target(z, x, y, c))))
    return lax.ppermute(block, AXES, route)


def product_kernel(pos, *refs):
    row_refs = refs[:NZ]
    whole_ref, out_ref, a_buf, w_buf, a_sem, w_sem = refs[NZ:]
    m, c = pos[1], pos[2]
    y = lax.div(m, NC)
    copies = []
    for j in range(NZ):
        core = c if j < NY else 1 - c
        from_y = lax.rem(y - SHIFTS[j % NY] + NY, NY)
        slot = lax.rem(NC * from_y + core + m, NZ)
        copies.append(
            (
                pltpu.make_async_copy(row_refs[j], a_buf.at[j], a_sem.at[j]),
                pltpu.make_async_copy(whole_ref.at[slot], w_buf.at[j], w_sem.at[j]),
            )
        )
    for rows, weight in copies:
        rows.start()
        weight.start()
    total = None
    for j, (rows, weight) in enumerate(copies):
        rows.wait()
        weight.wait()
        part = dot(a_buf[j], w_buf[j], 1, 1)
        total = part if total is None else total + part
    out_ref[...] = total.astype(BF16)


def product_call(pos, rows, whole):
    count, width = rows[0].shape
    n_rows = whole.shape[1]
    anywhere = pl.BlockSpec(memory_space=pl.ANY)
    return pl.pallas_call(
        product_kernel,
        grid_spec=pltpu.PrefetchScalarGridSpec(
            num_scalar_prefetch=1,
            grid=(1,),
            in_specs=[anywhere] * (len(rows) + 1),
            out_specs=pl.BlockSpec((count, n_rows), lambda i, p: (0, 0)),
            scratch_shapes=[
                pltpu.VMEM((NZ, count, width), BF16),
                pltpu.VMEM((NZ, n_rows, width), BF16),
                pltpu.SemaphoreType.DMA((NZ,)),
                pltpu.SemaphoreType.DMA((NZ,)),
            ],
        ),
        out_shape=jax.ShapeDtypeStruct((count, n_rows), BF16),
        name="byte_product",
        compiler_params=pltpu.CompilerParams(vmem_limit_bytes=40 << 20),
    )(pos, *in_hbm(*rows, whole))


def local(
    win_query, win_key, win_value, win_dout, cross_query, cross_dout,
    patch_key, patch_value, patch_len, patch_owner, w_query,
):
    z, x = lax.axis_index("z"), lax.axis_index("x")
    y, core = lax.axis_index("y"), lax.axis_index("core")
    seq_count = NZ * NX
    seq_index = z * NX + x
    flags = jnp.stack([seq_index > 0, seq_index == seq_count - 1]).astype(jnp.int32)
    pos = jnp.stack([x, y * NC + core, core]).astype(jnp.int32)
    own = send(w_query, lambda z, x, y, c: (z + NC * y + c, x, z // NC, z % NC))
    low_rim, high_rim = pack_call(win_key, win_value)
    own, low_rim, high_rim, cross_query = lax.optimization_barrier(
        (own, low_rim, high_rim, cross_query)
    )
    whole = lax.all_gather(own, SEQ, axis=0, tiled=True)
    whole = whole.reshape(NZ, NX * own.shape[0], own.shape[1])
    cross_dq, buffer = cross_call(
        cross_query, cross_dout, patch_key, patch_value, patch_len, patch_owner, seq_count, 1
    )
    before = shifted(low_rim, SEQ, 1)
    after = shifted(high_rim, SEQ, -1)
    cross_dq = cross_dq.reshape(cross_dq.shape[1:])
    rows = [cross_dq] + [
        send(cross_dq, lambda z, x, y, c, dy=dy: (z, x, y + dy, c)) for dy in SHIFTS[1:]
    ]
    win_dq, dk, dv, low_send, high_send = window_call(
        flags, win_query, win_dout, win_key, win_value, before, after
    )
    win_dq, buffer = lax.optimization_barrier((win_dq, buffer))
    arrived = lax.all_to_all(buffer, SEQ, split_axis=0, concat_axis=0, tiled=True)
    rows, win_dq = lax.optimization_barrier((rows, win_dq))
    rows = rows + [send(r, lambda z, x, y, c: (z, x, y, 1 - c)) for r in rows]
    rows, low_send, high_send = lax.optimization_barrier((rows, low_send, high_send))
    low_back = shifted(low_send, SEQ, -1)
    high_back = shifted(high_send, SEQ, 1)
    win_dk, win_dv = join_call(dk, dv, low_back, high_back)
    patch_grads = arrived.transpose(1, 0, 2, 3).reshape(2, -1, arrived.shape[3])
    byte_grads = product_call(pos, rows, whole)
    return (win_dq, win_dk, win_dv, patch_grads, byte_grads)


def solution(mesh):
    mesh = Mesh(mesh.devices.reshape(NZ, NX, NY, NC), AXES)
    mp = ("y", "core")
    tile = P(SEQ, mp)
    rows = P(SEQ, None)
    in_specs = (tile,) * 8 + (rows, rows, tile)
    out_specs = (tile, tile, tile, P(None, SEQ, mp), tile)
    return jax.shard_map(local, mesh=mesh, in_specs=in_specs, out_specs=out_specs, check_vma=False)
```

```python
import functools
import math

import jax
import jax.numpy as jnp
from jax import lax
from jax.experimental import pallas as pl
from jax.experimental.pallas import tpu as pltpu
from jax.sharding import Mesh
from jax.sharding import PartitionSpec as P

HD = 128
WIN = 256
INV_ROOT = 1.0 / math.sqrt(HD)
F32 = jnp.float32
BF16 = jnp.bfloat16


def dot(a, b, ca, cb):
    return lax.dot_general(a, b, (((ca,), (cb,)), ((), ())), preferred_element_type=F32)


def in_hbm(*arrays):
    return [pltpu.with_memory_space_constraint(a, pltpu.HBM) for a in arrays]


def window_block(q, do, k_rim, v_rim, k_own, v_own, rim_ok, own_ok):
    s_rim = jnp.where(rim_ok, dot(k_rim, q, 1, 1), -1e30)
    s_own = jnp.where(own_ok, dot(k_own, q, 1, 1), -1e30)
    top = jnp.maximum(
        jnp.max(s_rim, axis=0, keepdims=True), jnp.max(s_own, axis=0, keepdims=True)
    )
    e_rim = jnp.exp((s_rim - top) * INV_ROOT)
    e_own = jnp.exp((s_own - top) * INV_ROOT)
    scale = 1.0 / (
        jnp.sum(e_rim, axis=0, keepdims=True) + jnp.sum(e_own, axis=0, keepdims=True)
    )
    d_rim = dot(v_rim, do, 1, 1)
    d_own = dot(v_own, do, 1, 1)
    p_rim = e_rim * scale
    p_own = e_own * scale
    delta = jnp.sum(p_rim * d_rim, axis=0, keepdims=True) + jnp.sum(
        p_own * d_own, axis=0, keepdims=True
    )
    g_rim = (p_rim * (d_rim - delta) * INV_ROOT).astype(BF16)
    g_own = (p_own * (d_own - delta) * INV_ROOT).astype(BF16)
    p_rim = p_rim.astype(BF16)
    p_own = p_own.astype(BF16)
    dq = dot(g_rim, k_rim, 0, 0) + dot(g_own, k_own, 0, 0)
    return (
        dq,
        dot(g_rim, q, 1, 0),
        dot(p_rim, do, 1, 0),
        dot(g_own, q, 1, 0),
        dot(p_own, do, 1, 0),
    )


def window_kernel(
    flags, q_ref, do_ref, k_ref, v_ref, before_ref, after_ref,
    dq_ref, dk_ref, dv_ref, low_ref, high_ref,
):
    low_valid = flags[0]
    is_last = flags[1]
    rows = lax.broadcasted_iota(jnp.int32, (WIN, WIN), 0)
    cols = lax.broadcasted_iota(jnp.int32, (WIN, WIN), 1)
    rim_ok = rows >= cols
    own_ok = rows <= cols
    lo = slice(0, WIN)
    hi = slice(WIN, 2 * WIN)
    k_low, v_low = k_ref[lo, :], v_ref[lo, :]
    dq, dk_r, dv_r, dk_low, dv_low = window_block(
        q_ref[lo, :], do_ref[lo, :], before_ref[0], before_ref[1], k_low, v_low,
        rim_ok & (low_valid > 0), own_ok,
    )
    dq_ref[lo, :] = dq.astype(BF16)
    low_ref[0] = dk_r.astype(BF16)
    low_ref[1] = dv_r.astype(BF16)
    last = is_last > 0
    k_prev = jnp.where(last, k_low, after_ref[0])
    v_prev = jnp.where(last, v_low, after_ref[1])
    dq, dk_r, dv_r, dk_own, dv_own = window_block(
        q_ref[hi, :], do_ref[hi, :], k_prev, v_prev, k_ref[hi, :], v_ref[hi, :],
        rim_ok, own_ok,
    )
    dq_ref[hi, :] = dq.astype(BF16)
    high_ref[0] = dk_r.astype(BF16)
    high_ref[1] = dv_r.astype(BF16)
    dk_ref[hi, :] = dk_own
    dv_ref[hi, :] = dv_own
    dk_ref[lo, :] = dk_low + jnp.where(last, dk_r, 0.0)
    dv_ref[lo, :] = dv_low + jnp.where(last, dv_r, 0.0)


def window_call(flags, q, do, k, v, before, after):
    rows, width = q.shape
    full = pl.BlockSpec((rows, HD), lambda h, f: (0, h))
    rim = pl.BlockSpec((2, WIN, HD), lambda h, f: (0, 0, h))
    return pl.pallas_call(
        window_kernel,
        grid_spec=pltpu.PrefetchScalarGridSpec(
            num_scalar_prefetch=1,
            grid=(width // HD,),
            in_specs=[full] * 4 + [rim] * 2,
            out_specs=[full, full, full, rim, rim],
        ),
        out_shape=(
            jax.ShapeDtypeStruct((rows, width), BF16),
            jax.ShapeDtypeStruct((rows, width), F32),
            jax.ShapeDtypeStruct((rows, width), F32),
            jax.ShapeDtypeStruct((2, WIN, width), BF16),
            jax.ShapeDtypeStruct((2, WIN, width), BF16),
        ),
        name="window_grads",
        cost_estimate=pl.CostEstimate(flops=8_000_000_000, transcendentals=0, bytes_accessed=25_000_000),
        compiler_params=pltpu.CompilerParams(vmem_limit_bytes=40 << 20),
    )(flags, *in_hbm(q, do, k, v, before, after))


def cross_kernel(q_ref, do_ref, k_ref, v_ref, len_ref, owner_ref, dq_ref, buf_ref, sel_ref):
    blocks = len_ref.shape[0]
    per_block = len_ref.shape[1]
    rows = q_ref.shape[0] // blocks
    patches = blocks * per_block
    slots = sel_ref.shape[0]
    cap = buf_ref.shape[2]

    @pl.when(pl.program_id(0) == 0)
    def _():
        owner_col = jnp.broadcast_to(owner_ref[...], (patches, patches))
        owner_row = owner_col.T
        earlier = lax.broadcasted_iota(
            jnp.int32, (patches, patches), 0
        ) < lax.broadcasted_iota(jnp.int32, (patches, patches), 1)
        same = jnp.where((owner_col == owner_row) & earlier, 1, 0)
        rank = jnp.sum(same, axis=0, keepdims=True)
        slot = owner_ref[...] * cap + rank
        at = lax.broadcasted_iota(jnp.int32, (slots, patches), 0)
        sel_ref[...] = jnp.where(at == slot, 1.0, 0.0).astype(BF16)

    before = lax.broadcasted_iota(
        jnp.int32, (per_block, per_block), 1
    ) < lax.broadcasted_iota(jnp.int32, (per_block, per_block), 0)
    starts = dot(
        jnp.where(before, 1.0, 0.0).astype(BF16), len_ref[...].astype(F32).astype(BF16), 1, 1
    ).astype(jnp.int32)
    within = lax.broadcasted_iota(jnp.int32, (per_block, rows), 1)
    dks, dvs = [], []
    for b in range(blocks):
        r = slice(b * rows, (b + 1) * rows)
        p = slice(b * per_block, (b + 1) * per_block)
        q, do, k, v = q_ref[r, :], do_ref[r, :], k_ref[p, :], v_ref[p, :]
        ok = starts[:, b : b + 1] <= within
        s = jnp.where(ok, dot(k, q, 1, 1), -1e30)
        e = jnp.exp((s - jnp.max(s, axis=0, keepdims=True)) * INV_ROOT)
        probs = e * (1.0 / jnp.sum(e, axis=0, keepdims=True))
        d = dot(v, do, 1, 1)
        delta = jnp.sum(probs * d, axis=0, keepdims=True)
        g = (probs * (d - delta) * INV_ROOT).astype(BF16)
        dq = dot(g, k, 0, 0).astype(BF16)
        for i in range(dq_ref.shape[0]):
            dq_ref[i, r, :] = dq
        dks.append(dot(g, q, 1, 0).astype(BF16))
        dvs.append(dot(probs.astype(BF16), do, 1, 0).astype(BF16))
    sel = sel_ref[...]
    for i, parts in enumerate((dks, dvs)):
        placed = dot(sel, jnp.concatenate(parts, axis=0), 1, 0).astype(BF16)
        buf_ref[:, i] = placed.reshape(slots // cap, cap, HD)


def cross_call(q, do, k, v, lens, owners, owner_count, copies):
    rows, width = q.shape
    patches = k.shape[0]
    cap = max(2, 2 * (patches // owner_count))
    col = pl.BlockSpec((rows, HD), lambda h: (0, h))
    pcol = pl.BlockSpec((patches, HD), lambda h: (0, h))
    return pl.pallas_call(
        cross_kernel,
        grid_spec=pltpu.PrefetchScalarGridSpec(
            num_scalar_prefetch=0,
            grid=(width // HD,),
            in_specs=[
                col, col, pcol, pcol,
                pl.BlockSpec(lens.shape, lambda h: (0, 0)),
                pl.BlockSpec((1, patches), lambda h: (0, 0)),
            ],
            out_specs=[
                pl.BlockSpec((copies, rows, HD), lambda h: (0, 0, h)),
                pl.BlockSpec((owner_count, 2, cap, HD), lambda h: (0, 0, 0, h)),
            ],
            scratch_shapes=[pltpu.VMEM((owner_count * cap, patches), BF16)],
        ),
        out_shape=(
            jax.ShapeDtypeStruct((copies, rows, width), BF16),
            jax.ShapeDtypeStruct((owner_count, 2, cap, width), BF16),
        ),
        name="cross_grads",
        cost_estimate=pl.CostEstimate(flops=5_000_000_000, transcendentals=0, bytes_accessed=15_000_000),
        compiler_params=pltpu.CompilerParams(vmem_limit_bytes=40 << 20),
    )(*in_hbm(q, do, k, v, lens, owners.reshape(1, patches)))


def join_kernel(dk_ref, dv_ref, low_ref, high_ref, dk_out, dv_out):
    for i, (src, out) in enumerate(((dk_ref, dk_out), (dv_ref, dv_out))):
        out[:WIN, :] = (src[:WIN, :] + low_ref[i].astype(F32)).astype(BF16)
        out[WIN:, :] = (src[WIN:, :] + high_ref[i].astype(F32)).astype(BF16)


def join_call(dk, dv, low_back, high_back):
    rows, width = dk.shape
    step = 2 * HD
    col = pl.BlockSpec((rows, step), lambda h: (0, h))
    rim = pl.BlockSpec((2, WIN, step), lambda h: (0, 0, h))
    out = jax.ShapeDtypeStruct((rows, width), BF16)
    return pl.pallas_call(
        join_kernel,
        grid=(width // step,),
        in_specs=[col, col, rim, rim],
        out_specs=[col, col],
        out_shape=(out, out),
        name="join_rims",
        compiler_params=pltpu.CompilerParams(vmem_limit_bytes=40 << 20),
    )(*in_hbm(dk, dv, low_back, high_back))


def pack_kernel(k_ref, v_ref, low_ref, high_ref):
    for i, ref in enumerate((k_ref, v_ref)):
        low_ref[i] = ref[:WIN, :]
        high_ref[i] = ref[WIN:, :]


def pack_call(k, v):
    rows, width = k.shape
    step = 2 * HD
    full = pl.BlockSpec((rows, step), lambda h: (0, h))
    rim = pl.BlockSpec((2, WIN, step), lambda h: (0, 0, h))
    out = jax.ShapeDtypeStruct((2, WIN, width), BF16)
    return pl.pallas_call(
        pack_kernel,
        grid=(width // step,),
        in_specs=[full] * 2,
        out_specs=[rim, rim],
        out_shape=(out, out),
        name="pack_rims",
    )(*in_hbm(k, v))


def shifted(block, axis, distance):
    devices = range(lax.axis_size(axis))
    route = [(i - distance, i) for i in devices if i - distance in devices]
    return lax.ppermute(block, axis, route)


NZ, NX, NY, NC = 8, 4, 4, 2
AXES = ("z", "x", "y", "core")
SEQ = ("z", "x")


def place(z, x, y, c):
    return ((z % NZ) * NX + x % NX) * (NY * NC) + (y % NY) * NC + c


def send(block, target):
    route = []
    for z in range(NZ):
        for x in range(NX):
            for y in range(NY):
                for c in range(NC):
                    route.append((place(z, x, y, c), place(*target(z, x, y, c))))
    return lax.ppermute(block, AXES, route)


def product_kernel(
    pos, own_ref, other_ref, whole_ref, out_ref, a_buf, w_buf, a_sem, w_sem
):
    m, c = pos[1], pos[2]
    copies = []
    for j in range(NZ):
        rows, core = (own_ref, c) if j % NC == 0 else (other_ref, 1 - c)
        slot = lax.rem(NC * (j // NC) + core + m, NZ)
        copies.append(
            (
                pltpu.make_async_copy(rows.at[j // NC], a_buf.at[j], a_sem.at[j]),
                pltpu.make_async_copy(whole_ref.at[slot], w_buf.at[j], w_sem.at[j]),
            )
        )
    for rows, weight in copies:
        rows.start()
        weight.start()
    total = None
    for j, (rows, weight) in enumerate(copies):
        rows.wait()
        weight.wait()
        part = dot(a_buf[j], w_buf[j], 1, 1)
        total = part if total is None else total + part
    out_ref[...] = total.astype(BF16)


def product_call(pos, own_rows, other_rows, whole):
    count, width = own_rows.shape[1:]
    n_rows = whole.shape[1]
    anywhere = pl.BlockSpec(memory_space=pl.ANY)
    return pl.pallas_call(
        product_kernel,
        grid_spec=pltpu.PrefetchScalarGridSpec(
            num_scalar_prefetch=1,
            grid=(1,),
            in_specs=[anywhere] * 3,
            out_specs=pl.BlockSpec((count, n_rows), lambda i, p: (0, 0)),
            scratch_shapes=[
                pltpu.VMEM((NZ, count, width), BF16),
                pltpu.VMEM((NZ, n_rows, width), BF16),
                pltpu.SemaphoreType.DMA((NZ,)),
                pltpu.SemaphoreType.DMA((NZ,)),
            ],
        ),
        out_shape=jax.ShapeDtypeStruct((count, n_rows), BF16),
        name="byte_product",
        compiler_params=pltpu.CompilerParams(vmem_limit_bytes=40 << 20),
    )(pos, *in_hbm(own_rows, other_rows, whole))


def local(
    win_query, win_key, win_value, win_dout, cross_query, cross_dout,
    patch_key, patch_value, patch_len, patch_owner, w_query,
):
    z, x = lax.axis_index("z"), lax.axis_index("x")
    y, core = lax.axis_index("y"), lax.axis_index("core")
    seq_count = NZ * NX
    seq_index = z * NX + x
    flags = jnp.stack([seq_index > 0, seq_index == seq_count - 1]).astype(jnp.int32)
    pos = jnp.stack([x, y * NC + core, core]).astype(jnp.int32)
    own = send(w_query, lambda z, x, y, c: (z + NC * y + c, x, z // NC, z % NC))
    low_rim, high_rim = pack_call(win_key, win_value)
    cross_query, low_rim = lax.optimization_barrier((cross_query, low_rim))
    cross_dq, buffer = cross_call(
        cross_query, cross_dout, patch_key, patch_value, patch_len, patch_owner, seq_count, NY
    )
    own, cross_dq, buffer, low_rim, high_rim = lax.optimization_barrier(
        (own, cross_dq, buffer, low_rim, high_rim)
    )
    whole = lax.all_gather(own, SEQ, axis=0, tiled=True)
    whole = whole.reshape(NZ, NX * own.shape[0], own.shape[1])
    before = shifted(low_rim, SEQ, 1)
    after = shifted(high_rim, SEQ, -1)
    own_rows = lax.all_to_all(cross_dq, "y", split_axis=0, concat_axis=0, tiled=True)
    win_dq, dk, dv, low_send, high_send = window_call(
        flags, win_query, win_dout, win_key, win_value, before, after
    )
    arrived = lax.all_to_all(buffer, SEQ, split_axis=0, concat_axis=0, tiled=True)
    low_back = shifted(low_send, SEQ, -1)
    high_back = shifted(high_send, SEQ, 1)
    low_back, high_back, arrived, own_rows = lax.optimization_barrier(
        (low_back, high_back, arrived, own_rows)
    )
    other_rows = send(own_rows, lambda z, x, y, c: (z, x, y, 1 - c))
    win_dk, win_dv = join_call(dk, dv, low_back, high_back)
    patch_grads = arrived.transpose(1, 0, 2, 3).reshape(2, -1, arrived.shape[3])
    byte_grads = product_call(pos, own_rows, other_rows, whole)
    return (win_dq, win_dk, win_dv, patch_grads, byte_grads)


def solution(mesh):
    mesh = Mesh(mesh.devices.reshape(NZ, NX, NY, NC), AXES)
    mp = ("y", "core")
    tile = P(SEQ, mp)
    rows = P(SEQ, None)
    in_specs = (tile,) * 8 + (rows, rows, tile)
    out_specs = (tile, tile, tile, P(None, SEQ, mp), tile)
    return jax.shard_map(local, mesh=mesh, in_specs=in_specs, out_specs=out_specs, check_vma=False)
```
